512 devices in a mesh: dp: 8 (over y, core), expert: 64 (over x, z).
Axes of the slice: x: 4, y: 4, z: 16, core: 2. Of those that a mesh axis runs over, the one named last changes fastest.
Arguments:
- attn: bfloat16 [64, 256, 4096], P('expert', None, 'dp'), may hold values from -6 to 6
- resid: bfloat16 [64, 256, 2048], P('expert', 'dp'), may hold values from -6 to 6
- w_out: bfloat16 [4096, 2048], P('dp', 'expert'), may hold values from -0.09375 to 0.09375
- gain_post: float32 [2048], replicated, may hold values from 0.1 to 1.9
- route_ids: int32 [64, 256, 8], P('expert', 'dp'), may hold values from 0 to 63, all different within a row; in each aligned block of 32 rows (0 to 31, 32 to 63, ..., all dimensions but the last counted through in order) at most 8 rows name the same one
- route_logits: float32 [64, 256, 8], P('expert', 'dp'), may hold values from -2 to 260
- live_count: int32 [64, 8], P('expert', 'dp'), may hold values from 1 to 32, as said below
- w_gate_up: bfloat16 [64, 2048, 1536], P('expert', 'dp'), may hold values from -0.125 to 0.125
- w_down: bfloat16 [64, 768, 2048], P('expert', None, 'dp'), may hold values from -0.21875 to 0.21875
- gain_final: float32 [2048], replicated, may hold values from 0.1 to 1.9
Outputs:
- stream_out: bfloat16 [64, 256, 2048], P('expert', 'dp')
- normed_out: bfloat16 [64, 256, 2048], P('expert', 'dp')
The draws below stay inside these ranges and needn't reach their ends.
Inputs may be any that keep to these rules, and one draw needn't show every extreme that they name: `route_ids`: each row names 8 different experts; among the rows of one device no expert is named more than 8 times. `live_count`: the devices whose dp index is a multiple of 3 hold prefill rows, all live; the others hold decode rows with a varying count.
All inputs are finite; a program needn't handle non-finite values.
Results may differ from the reference program's by a relative error of at most 0.018.
Values may be sent and summed in bfloat16 or wider, within the bound.
A program may use at most 64 MiB of HBM per device.

```python
import math
import jax
import jax.numpy as jnp
import numpy as np
from jax import lax

D = 2048
F = 4096
FF = 768
TOP = 8
ROWS_DEV = 32
EXPERTS = 64
GROUPS = 64
ROWS_GRP = 256
CAP = 8
N_DP = 8


def draw_route_logits(key, part):
    first = jax.random.fold_in(key, 0)
    return jnp.clip(0.6 * jax.random.normal(first, (GROUPS, ROWS_GRP, TOP), jnp.float32), -1.8, 1.8)


def draw_live_count(key, part):
    counted = jax.random.randint(key, (GROUPS, N_DP), 1, ROWS_DEV + 1)
    dp_place = jnp.arange(N_DP)[None, :]
    return jnp.where(dp_place % 3 == 0, ROWS_DEV, counted).astype(jnp.int32)


def block_scale(key, extent, cuts, smallest, largest):
    factor_of, own = 1.0, jax.random.fold_in(key, 6)
    for axis_at, parts in cuts:
        draws = jnp.exp(jax.random.uniform(jax.random.fold_in(own, axis_at), (parts,), jnp.float32, smallest / len(cuts), largest / len(cuts)))
        factor_of = factor_of * jnp.repeat(draws, extent[axis_at] // parts).reshape([-1 if axis == axis_at else 1 for axis in range(len(extent))])
    return factor_of


def routed_block(key, own, number, rows, amount, top, reach, lean):
    order = jax.random.permutation(key, amount)
    crowded, common = load_shares(amount, rows * top, reach, lean, True), load_shares(amount, rows * top, reach, lean, False)
    places = jnp.arange(amount)

    def named(sizes, offset_by):
        used = int((sizes > 0).sum())
        fixed = max(1, used // 4)
        passed = fixed + (places - fixed + offset_by * (used - fixed)) % max(1, amount - fixed)
        return jnp.zeros((amount,), jnp.int32).at[order[jnp.where(places < fixed, places, passed)]].set(jnp.asarray(sizes, jnp.int32))

    sizes = jnp.where(number % 4 == 0, named(crowded, number // 4), named(common, number - number // 4 - 1))
    mixed = jax.random.permutation(jax.random.fold_in(own, 3), amount)
    donor, taker = mixed[0:amount // 2 * 2:2], mixed[1:amount // 2 * 2:2]
    margin = jnp.minimum(sizes[donor] - 1, reach - sizes[taker]) // 2
    margin = jnp.where((donor == order[0]) | (taker == order[0]) | (sizes[taker] == 0), 0, jnp.maximum(margin, 0))
    passed = jax.random.randint(jax.random.fold_in(own, 4), (amount // 2,), 0, 1 << 20) % (margin + 1)
    sizes = sizes.at[donor].add(-passed).at[taker].add(passed)
    members = jnp.searchsorted(jnp.cumsum(sizes), jnp.arange(rows * top), side="right").astype(jnp.int32)
    listing = members.reshape(top, rows).T
    listing = listing[jax.random.permutation(jax.random.fold_in(own, 1), rows)]
    offset_by = jax.random.randint(jax.random.fold_in(own, 2), (rows, 1), 0, top)
    return jnp.take_along_axis(listing, (jnp.arange(top)[None, :] + offset_by) % top, axis=1)


def load_shares(number_of, total, reach, slope, full):
    loads = [(1 << 20) // math.isqrt(standing ** slope) + 1 for standing in range(1, number_of + 1)]
    largest = reach if full else min(reach, max(-(-total // number_of), total * loads[0] // sum(loads)))
    least = 1 if total - largest >= number_of - 1 else 0
    given, spare = [largest] + [least] * (number_of - 1), total - largest - least * (number_of - 1)
    while spare > 0:
        candidates = [i for i in range(1, number_of) if given[i] < largest] or [i for i in range(1, number_of) if given[i] < reach]
        whole, remaining = sum([loads[i] for i in candidates]), spare
        for i in candidates:
            extra = min(reach - given[i], max(1, remaining * loads[i] // whole), spare)
            given[i] = given[i] + extra
            spare = spare - extra
    return np.array(given)


def scatter_about(stream_key, extent, deviation, limit, cuts=(), kind=jnp.bfloat16):
    level = block_scale(stream_key, extent, cuts, -0.22, 0.18) if cuts else 1.0
    entries = jax.random.normal(stream_key, extent, jnp.float32) * deviation * level
    return jnp.minimum(jnp.maximum(entries, -limit), limit).astype(kind)


def setup_inputs(seed: int = 0) -> dict:
    keys = jax.random.split(jax.random.key(seed), 11)
    attn = scatter_about(keys[0], (GROUPS, ROWS_GRP, F), 1.0, 6.0, ((0, 64), (2, 8)))
    resid = scatter_about(keys[1], (GROUPS, ROWS_GRP, D), 1.0, 6.0, ((0, 64), (1, 8)))
    w_out = scatter_about(keys[2], (F, D), F ** -0.5, 0.09375, ((0, 8), (1, 64)))
    gain_post = jnp.clip(1.0 + 0.18 * jax.random.normal(keys[3], (D,), jnp.float32), 0.1, 1.9)
    route_ids_keys = jax.random.split(jax.random.fold_in(keys[4], 1), GROUPS * ROWS_GRP // ROWS_DEV)
    route_ids_turns = jax.random.permutation(jax.random.fold_in(keys[4], 3), GROUPS * ROWS_GRP // ROWS_DEV)
    route_ids = jax.vmap(lambda own, number: routed_block(jax.random.fold_in(keys[4], 2), own, number, ROWS_DEV, EXPERTS, TOP, CAP, 2))(route_ids_keys, route_ids_turns).reshape((GROUPS, ROWS_GRP, TOP))
    route_logits = draw_route_logits(jax.random.fold_in(keys[10], 71), 0)
    live_count = draw_live_count(jax.random.fold_in(keys[10], 71), 0)
    w_gate_up = scatter_about(keys[7], (EXPERTS, D, 2 * FF), D ** -0.5, 0.125, ((0, 64), (1, 8)))
    w_down = scatter_about(keys[8], (EXPERTS, FF, D), FF ** -0.5, 0.21875, ((0, 64), (2, 8)))
    gain_final = jnp.clip(1.0 + 0.18 * jax.random.normal(keys[9], (D,), jnp.float32), 0.1, 1.9)
    return {"attn": attn, "resid": resid, "w_out": w_out, "gain_post": gain_post, "route_ids": route_ids, "route_logits": route_logits, "live_count": live_count, "w_gate_up": w_gate_up, "w_down": w_down, "gain_final": gain_final}


def rms_scale(values, gain):
    return values * lax.rsqrt(lax.optimization_barrier(jnp.mean(values * values, axis=-1, keepdims=True)) + 1e-06) * gain

def reference(attn, resid, w_out, gain_post, route_ids, route_logits, live_count, w_gate_up, w_down, gain_final):
    row_total = GROUPS * ROWS_GRP
    feat_block = F // N_DP
    proj = jnp.zeros((row_total, D), jnp.float32)
    for blk in range(N_DP):
        part = attn[:, :, blk * feat_block:(blk + 1) * feat_block].reshape(row_total, feat_block)
        term = jnp.dot(part, w_out[blk * feat_block:(blk + 1) * feat_block], preferred_element_type=jnp.float32)
        term = lax.optimization_barrier(term.astype(jnp.bfloat16))
        proj = proj + term.astype(jnp.float32)
    stream_in = (resid.reshape(row_total, D).astype(jnp.float32) + proj).astype(jnp.bfloat16)
    stream_float = stream_in.astype(jnp.float32)
    normed_in = rms_scale(stream_float, gain_post).astype(jnp.bfloat16)
    probs = jax.nn.softmax(route_logits.reshape(row_total, TOP).astype(jnp.float32), axis=-1).astype(jnp.bfloat16)
    position = jnp.arange(ROWS_GRP, dtype=jnp.int32)
    device_row = position // ROWS_DEV
    within = position % ROWS_DEV
    alive = (within[None, :] < live_count[:, device_row]).reshape(row_total)
    weights = (probs.astype(jnp.float32) * alive[:, None].astype(jnp.float32)).reshape(-1)
    block_len = 256
    route_total = row_total * TOP
    chosen = route_ids.reshape(route_total).astype(jnp.int32)
    order = jnp.argsort(chosen, stable=True).astype(jnp.int32)
    sorted_ids = chosen[order]
    counts = lax.optimization_barrier(jnp.sum((chosen[:, None] == jnp.arange(EXPERTS, dtype=jnp.int32)[None, :]).astype(jnp.int32), axis=0))
    starts = jnp.cumsum(counts) - counts
    padded = (counts + block_len - 1) // block_len * block_len
    pad_start = jnp.cumsum(padded) - padded
    pad_end = pad_start + padded
    slot_pos = (pad_start[sorted_ids] + jnp.arange(route_total, dtype=jnp.int32) - starts[sorted_ids]).astype(jnp.int32)
    block_count = (route_total + block_len - 1) // block_len + EXPERTS
    slot_route = jnp.full((block_count * block_len,), -1, jnp.int32).at[slot_pos].set(order)
    block_first = jnp.arange(block_count, dtype=jnp.int32) * block_len
    block_expert = jnp.minimum(lax.optimization_barrier(jnp.sum((block_first[:, None] >= pad_end[None, :]).astype(jnp.int32), axis=1)), EXPERTS - 1).astype(jnp.int32)

    def one_block(mixture, block):
        routes = lax.dynamic_slice_in_dim(slot_route, block * block_len, block_len)
        valid = routes >= 0
        route = jnp.where(valid, routes, 0)
        row = route // TOP
        rows_in = normed_in[row]
        expert = block_expert[block]
        gate_up = lax.dynamic_index_in_dim(w_gate_up, expert, 0, keepdims=False)
        down = lax.dynamic_index_in_dim(w_down, expert, 0, keepdims=False)
        both = jnp.dot(rows_in, gate_up, preferred_element_type=jnp.float32)
        inner = (jax.nn.silu(both[:, :FF]) * both[:, FF:]).astype(jnp.bfloat16)
        expert_out = jnp.dot(inner, down, preferred_element_type=jnp.float32).astype(jnp.bfloat16)
        scale = jnp.where(valid, weights[route], jnp.float32(0.0))
        mixture = mixture.at[row].add(scale[:, None] * expert_out.astype(jnp.float32))
        return (mixture, None)
    mixture, unused = lax.scan(one_block, jnp.zeros((row_total, D), jnp.float32), jnp.arange(block_count, dtype=jnp.int32))
    stream_out = (stream_float + mixture).astype(jnp.bfloat16)
    normed_out = rms_scale(stream_out.astype(jnp.float32), gain_final).astype(jnp.bfloat16)
    return (stream_out.reshape(GROUPS, ROWS_GRP, D), normed_out.reshape(GROUPS, ROWS_GRP, D))
```

```python
import math

import jax
import jax.numpy as jnp
from jax import lax
from jax.experimental import pallas as pl
from jax.experimental.pallas import tpu as pltpu
from jax.sharding import PartitionSpec as P

NX, NZ, NY = 4, 16, 4
MESH = pl.DeviceIdType.MESH


def rms_scale(values, gain):
    return values * lax.rsqrt(jnp.mean(values * values, axis=-1, keepdims=True) + 1e-06) * gain


def swiglu_rows(rows_in, gate_up, down, hidden_units):
    both = jnp.dot(rows_in, gate_up, preferred_element_type=jnp.float32)
    inner = (jax.nn.silu(both[:, :hidden_units]) * both[:, hidden_units:]).astype(jnp.bfloat16)
    return jnp.dot(inner, down, preferred_element_type=jnp.float32).astype(jnp.bfloat16)


def places():
    dp = lax.axis_index("dp")
    expert = lax.axis_index("expert")
    return dp, expert // NZ, expert % NZ


def greet(dp, x, z):
    peers = [(dp, x * NZ + (z + 1) % NZ), (dp, x * NZ + (z + NZ - 1) % NZ)]
    peers += [(dp, (x + step) % NX * NZ + z) for step in range(1, NX)]
    peers += [((dp + step) % 8, x * NZ + z) for step in range(1, 8)]
    barrier = pltpu.get_barrier_semaphore()
    for peer in peers:
        pl.semaphore_signal(barrier, inc=1, device_id=peer, device_id_type=MESH)
    pl.semaphore_wait(barrier, len(peers))


def remote(src, dst, send_sem, recv_sem, peer):
    return pltpu.make_async_remote_copy(
        src_ref=src,
        dst_ref=dst,
        send_sem=send_sem,
        recv_sem=recv_sem,
        device_id=peer,
        device_id_type=MESH,
    )


def project_kernel(
    attn_ref,
    resid_ref,
    w_ref,
    gain_ref,
    stream_ref,
    normed_ref,
    wbuf,
    pbuf,
    rbuf,
    wz_send,
    wz_recv,
    wx_send,
    wx_recv,
    rs_send,
    rs_recv,
):
    dp, x, z = places()
    up, below = (dp, x * NZ + (z + 1) % NZ), (dp, x * NZ + (z + NZ - 1) % NZ)
    right, left = (dp, (x + 1) % NX * NZ + z), (dp, (x + NX - 1) % NX * NZ + z)
    greet(dp, x, z)
    wbuf[x * NZ + z] = w_ref[...]

    def block(column, side, h):
        return wbuf.at[(x + column) % NX * NZ + (z + (h if side == 0 else NZ - h)) % NZ]

    def z_copy(side, h):
        ref = block(0, side if h else 0, h)
        at = side * 8 + h
        return remote(ref, ref, wz_send.at[at], wz_recv.at[at], below if side == 0 else up)

    def z_arrival(side, h):
        ref = block(0, side, h)
        at = side * 8 + h - 1
        return remote(ref, ref, wz_send.at[at], wz_recv.at[at], below if side == 0 else up)

    def place(side, h):
        return h if side == 0 else 7 + h

    def x_copy(way, side, h):
        at = way * 16 + place(side, h)
        if way == 2:
            ref = block(1, side, h) if side == 0 else block(3, side, h)
            peer = left if side == 0 else right
        else:
            ref = block(0, side, h)
            peer = right if way == 0 else left
        return remote(ref, ref, wx_send.at[at], wx_recv.at[at], peer)

    def x_arrival(way, side, h):
        at = way * 16 + place(side, h)
        ref = block((3, 1, 2)[way], side, h)
        return remote(ref, ref, wx_send.at[at], wx_recv.at[at], right)

    def steps(h):
        return [(side, h) for side in (0, 1) if (side == 0 and h <= 7) or (side == 1 and h >= 1)]

    for h in range(9):
        if h == 0:
            z_copy(0, 0).start()
            z_copy(1, 0).start()
        for side, at in steps(h):
            if at:
                z_arrival(side, at).wait_recv()
                if at < (7 if side == 0 else 8):
                    z_copy(side, at).start()
            x_copy(0, side, at).start()
            x_copy(1, side, at).start()
        if h >= 2:
            for side, at in steps(h - 2):
                x_arrival(1 if side == 0 else 0, side, at).wait_recv()
                x_copy(2, side, at).start()
    for h in (7, 8):
        for side, at in steps(h):
            x_arrival(1 if side == 0 else 0, side, at).wait_recv()
            x_copy(2, side, at).start()

    every = [(side, h) for h in range(9) for side, _ in steps(h)]

    def rs_copy(step, order, column):
        target = (dp + step) % 8
        at = (step - 1) * 4 + order
        return remote(
            pbuf.at[column, target],
            rbuf.at[dp, column],
            rs_send.at[at],
            rs_recv.at[at],
            (target, x * NZ + z),
        )

    for order in range(4):
        column = (x + (0, 3, 1, 2)[order]) % NX
        if order:
            way = order - 1
            for side, h in every:
                if not (way == 0 and side == 1) and not (way == 1 and side == 0):
                    x_arrival(way, side, h).wait_recv()
        part = wbuf[pl.ds(column * NZ, NZ)].reshape(512, 512)
        got = lax.dot_general(
            attn_ref[...], part, (((1,), (1,)), ((), ())), preferred_element_type=jnp.float32
        )
        pbuf[column] = got.astype(jnp.bfloat16).reshape(8, 32, 512)
        for step in range(1, 8):
            rs_copy(step, order, column).start()

    for order in range(4):
        column = (x + (0, 3, 1, 2)[order]) % NX
        for step in range(1, 8):
            source = (dp + 8 - step) % 8
            at = (step - 1) * 4 + order
            remote(
                pbuf.at[column, source],
                rbuf.at[source, column],
                rs_send.at[at],
                rs_recv.at[at],
                (source, x * NZ + z),
            ).wait_recv()
        rbuf[dp, column] = pbuf[column, dp]

    square = jnp.zeros((32, 1), jnp.float32)
    for g in range(4):
        total = resid_ref[:, g * 512 : (g + 1) * 512].astype(jnp.float32)
        proj = rbuf[0, g].astype(jnp.float32)
        for source in range(1, 8):
            proj += rbuf[source, g].astype(jnp.float32)
        held = (total + proj).astype(jnp.bfloat16)
        stream_ref[:, g * 512 : (g + 1) * 512] = held
        wide = held.astype(jnp.float32)
        square += jnp.sum(wide * wide, axis=-1, keepdims=True)
    scale = lax.rsqrt(square / 2048.0 + 1e-06)
    normed_ref[...] = (stream_ref[...].astype(jnp.float32) * scale * gain_ref[...]).astype(jnp.bfloat16)

    z_copy(0, 0).wait_send()
    z_copy(1, 0).wait_send()
    for side, h in every:
        if h and h < (7 if side == 0 else 8):
            z_copy(side, h).wait_send()
        for way in range(3):
            x_copy(way, side, h).wait_send()
    for order in range(4):
        column = (x + (0, 3, 1, 2)[order]) % NX
        for step in range(1, 8):
            rs_copy(step, order, column).wait_send()


def project(attn, resid, w_rows, gain):
    vmem = pl.BlockSpec(memory_space=pltpu.VMEM)
    return pl.pallas_call(
        project_kernel,
        out_shape=[jax.ShapeDtypeStruct((32, 2048), jnp.bfloat16)] * 2,
        in_specs=[vmem] * 4,
        out_specs=[vmem] * 2,
        scratch_shapes=[
            pltpu.VMEM((64, 32, 512), jnp.bfloat16),
            pltpu.VMEM((4, 8, 32, 512), jnp.bfloat16),
            pltpu.VMEM((8, 4, 32, 512), jnp.bfloat16),
            pltpu.SemaphoreType.DMA((16,)),
            pltpu.SemaphoreType.DMA((16,)),
            pltpu.SemaphoreType.DMA((48,)),
            pltpu.SemaphoreType.DMA((48,)),
            pltpu.SemaphoreType.DMA((28,)),
            pltpu.SemaphoreType.DMA((28,)),
        ],
        compiler_params=pltpu.CompilerParams(
            collective_id=0, has_side_effects=True, vmem_limit_bytes=32 << 20
        ),
    )(attn, resid, w_rows, gain)


def body(
    attn,
    resid,
    w_out,
    gain_post,
    route_ids,
    route_logits,
    live_count,
    w_gate_up,
    w_down,
    gain_final,
):
    rows_here = resid.shape[1]
    model_width = resid.shape[2]
    top_count = route_ids.shape[2]
    dp_count = lax.axis_size("dp")
    expert_count = lax.axis_size("expert")
    hidden_units = w_down.shape[1]
    capacity = dp_count * max(1, 2 * rows_here * top_count // (expert_count * dp_count))
    slot_count = expert_count * capacity
    stream_in, normed_in = project(attn[0], resid[0], w_out.T, gain_post[None])
    stream_float = stream_in.astype(jnp.float32)
    probs = jax.nn.softmax(route_logits[0], axis=-1).astype(jnp.bfloat16)
    alive = jnp.arange(rows_here, dtype=jnp.int32) < live_count[0, 0]
    expert_of = route_ids[0].reshape(-1)
    route_alive = jnp.repeat(alive, top_count)
    onehot = (
        (expert_of[:, None] == jnp.arange(expert_count, dtype=jnp.int32)[None, :])
        & route_alive[:, None]
    ).astype(jnp.int32)
    earlier = jnp.sum((jnp.cumsum(onehot, axis=0) - onehot) * onehot, axis=1)
    target = expert_of * capacity + earlier
    match = (target[:, None] == jnp.arange(slot_count, dtype=jnp.int32)[None, :]) & route_alive[
        :, None
    ]
    placed = match.reshape(rows_here, top_count, slot_count)
    gather_matrix = jnp.any(placed, axis=1).astype(jnp.bfloat16)
    send_rows = lax.dot_general(
        gather_matrix, normed_in, (((0,), (0,)), ((), ())), preferred_element_type=jnp.float32
    ).astype(jnp.bfloat16)
    send_flags = jnp.sum(gather_matrix.astype(jnp.float32), axis=0).astype(jnp.bfloat16)
    combine_matrix = jnp.sum(
        jnp.where(placed, probs.astype(jnp.float32)[:, :, None], jnp.float32(0.0)), axis=1
    ).astype(jnp.bfloat16)
    arrived_rows, arrived_flags = (
        lax.all_to_all(
            send_rows.reshape(expert_count, capacity, model_width),
            "expert",
            split_axis=0,
            concat_axis=0,
            tiled=True,
        ),
        lax.all_to_all(
            send_flags.reshape(expert_count, capacity),
            "expert",
            split_axis=0,
            concat_axis=0,
            tiled=True,
        ),
    )
    arrived = arrived_rows.reshape(slot_count, model_width)
    flags = arrived_flags.reshape(slot_count)
    gate_up_full, down_full = (
        lax.all_gather(w_gate_up, "dp", axis=1, tiled=True),
        lax.all_gather(w_down, "dp", axis=2, tiled=True),
    )
    live_slot = (flags > 0.5).astype(jnp.int32)
    order = jnp.argsort(1 - live_slot, stable=True)
    live_total = jnp.sum(live_slot)
    packed = arrived[order]
    block_len = math.gcd(slot_count, 128)
    block_total = (live_total + block_len - 1) // block_len

    def run_block(index, outputs):
        begin = index * block_len
        rows_in = lax.dynamic_slice_in_dim(packed, begin, block_len, 0)
        block_out = swiglu_rows(rows_in, gate_up_full[0], down_full[0], hidden_units)
        return lax.dynamic_update_slice_in_dim(outputs, block_out, begin, 0)

    packed_out = lax.fori_loop(
        0, block_total, run_block, jnp.zeros((slot_count, model_width), jnp.bfloat16)
    )
    position = (
        jnp.zeros((slot_count,), jnp.int32).at[order].set(jnp.arange(slot_count, dtype=jnp.int32))
    )
    results = packed_out[position]
    returned = lax.all_to_all(
        results.reshape(expert_count, capacity, model_width),
        "expert",
        split_axis=0,
        concat_axis=0,
        tiled=True,
    )
    returned = returned.reshape(slot_count, model_width)
    mixture = jnp.dot(combine_matrix, returned, preferred_element_type=jnp.float32)
    stream_out = (stream_float + mixture).astype(jnp.bfloat16)
    normed_out = rms_scale(stream_out.astype(jnp.float32), gain_final).astype(jnp.bfloat16)
    return (stream_out[None], normed_out[None])


def solution(mesh):
    placed = (
        P("expert", None, "dp"),
        P("expert", "dp", None),
        P("dp", "expert"),
        P(),
        P("expert", "dp", None),
        P("expert", "dp", None),
        P("expert", "dp"),
        P("expert", "dp", None),
        P("expert", None, "dp"),
        P(),
    )
    return jax.shard_map(
        body,
        mesh=mesh,
        in_specs=placed,
        out_specs=(P("expert", "dp", None), P("expert", "dp", None)),
        check_vma=False,
    )
```

```python
import jax
import jax.numpy as jnp
from jax import lax
from jax.experimental import pallas as pl
from jax.experimental.pallas import tpu as pltpu
from jax.sharding import PartitionSpec as P

NX, NZ, NY, NC = 4, 16, 4, 2
NDP = NY * NC
ROWS, D, FB, FF, TOP, CAP = 32, 2048, 512, 768, 8, 8
GU_ROWS, DN_COLS, CUT = D // NDP, D // NDP, 192
PAIRS = NZ // 2
MESH = pl.DeviceIdType.MESH
F32, BF16 = jnp.float32, jnp.bfloat16
NT = (((1,), (1,)), ((), ()))


def remote(src, dst, send_sem, recv_sem, peer):
    return pltpu.make_async_remote_copy(
        src_ref=src,
        dst_ref=dst,
        send_sem=send_sem,
        recv_sem=recv_sem,
        device_id=peer,
        device_id_type=MESH,
    )


def ring_steps(h):
    return [side for side in (0, 1) if (side == 0 and h <= 7) or (side == 1 and h >= 1)]


def kernel(
    attn_ref,
    resid_ref,
    w_ref,
    gain_post_ref,
    ids_ref,
    logits_ref,
    live_ref,
    gate_up_ref,
    down_ref,
    gain_final_ref,
    stream_ref,
    normed_ref,
    wbuf,
    pbuf,
    rbuf,
    held,
    zbuf,
    cbuf,
    xbuf,
    inner,
    ybuf,
    ret,
    part,
    up_out,
    up_in,
    dn_out,
    dn_in,
    gu,
    dn,
    wz_send,
    wz_recv,
    wx_send,
    wx_recv,
    rs_send,
    rs_recv,
    own_sem,
    wt_send,
    wt_recv,
    nz_send,
    nz_recv,
    cx_send,
    cx_recv,
    yx_send,
    yx_recv,
    up_send,
    up_recv,
    dn_send,
    dn_recv,
):
    dp = lax.axis_index("dp")
    expert = lax.axis_index("expert")
    x, z = expert // NZ, expert % NZ
    y, core = dp // NC, dp % NC
    above, below = (dp, x * NZ + (z + 1) % NZ), (dp, x * NZ + (z + NZ - 1) % NZ)
    xpeer = [(dp, (x + step) % NX * NZ + z) for step in range(NX)]
    right, left = xpeer[1], xpeer[3]

    peers = [above, below] + xpeer[1:] + [((dp + step) % NDP, expert) for step in range(1, NDP)]
    barrier = pltpu.get_barrier_semaphore()
    for peer in peers:
        pl.semaphore_signal(barrier, inc=1, device_id=peer, device_id_type=MESH)
    pl.semaphore_wait(barrier, len(peers))

    wbuf[expert] = w_ref[...]

    def z_at(side, h):
        return (z + (h if side == 0 else NZ - h)) % NZ

    def w_block(column, side, h):
        return wbuf.at[(x + column) % NX * NZ + z_at(side, h)]

    def ring_copy(ref, side, h, send, recv):
        at = side * 8 + h
        return remote(ref, ref, send.at[at], recv.at[at], below if side == 0 else above)

    def wz_copy(side, h):
        return ring_copy(w_block(0, side, h), side, h, wz_send, wz_recv)

    def wz_arrival(side, h):
        return ring_copy(w_block(0, side, h), side, h - 1, wz_send, wz_recv)

    def place(side, h):
        return h if side == 0 else 7 + h

    def wx_copy(way, side, h):
        at = way * 16 + place(side, h)
        column = 0 if way < 2 else (1 if side == 0 else 3)
        peer = (right, left, left if side == 0 else right)[way]
        ref = w_block(column, side, h)
        return remote(ref, ref, wx_send.at[at], wx_recv.at[at], peer)

    def wx_arrival(way, side, h):
        at = way * 16 + place(side, h)
        ref = w_block((3, 1, 2)[way], side, h)
        return remote(ref, ref, wx_send.at[at], wx_recv.at[at], right)

    def w_forward(h):
        for side in ring_steps(h):
            wx_arrival(1 if side == 0 else 0, side, h).wait_recv()
            wx_copy(2, side, h).start()

    wz_copy(0, 0).start()
    wz_copy(1, 0).start()
    wx_copy(0, 0, 0).start()
    wx_copy(1, 0, 0).start()

    y_up, y_down = ((y + 1) % NY * NC + core, expert), ((y + NY - 1) % NY * NC + core, expert)
    sibling = (y * NC + 1 - core, expert)

    def piece(owner, number):
        if number == 2:
            return dn.at[owner]
        begin = pl.multiple_of(owner * GU_ROWS, GU_ROWS)
        return gu.at[pl.ds(begin, CUT)] if number == 0 else gu.at[pl.ds(begin + CUT, GU_ROWS - CUT)]

    def own_piece(number):
        if number == 2:
            return down_ref
        return gate_up_ref.at[pl.ds(0, CUT)] if number == 0 else gate_up_ref.at[pl.ds(CUT, GU_ROWS - CUT)]

    def owner_of(step, on_core):
        return (y + step) % NY * NC + on_core

    def wt(kind, number, src, dst, peer):
        at = kind * 3 + number
        return remote(src, dst, wt_send.at[at], wt_recv.at[at], peer)

    def weight_send(kind, number):
        if kind in (0, 1, 3):
            peer = {0: y_up, 1: y_down, 3: sibling}[kind]
            return wt(kind, number, own_piece(number), piece(dp, number), peer)
        if kind == 2:
            owner = owner_of(3 if number == 0 else 1, core)
            ref = piece(owner, number)
            return wt(kind, number, ref, ref, y_up if number == 0 else y_down)
        ref = piece(owner_of({4: 3, 5: 1, 6: 2}[kind], core), number)
        return wt(kind, number, ref, ref, sibling)

    def weight_arrival(kind, number):
        owner = {
            0: owner_of(3, core),
            1: owner_of(1, core),
            2: owner_of(2, core),
            3: owner_of(0, 1 - core),
            4: owner_of(3, 1 - core),
            5: owner_of(1, 1 - core),
            6: owner_of(2, 1 - core),
        }[kind]
        ref = piece(owner, number)
        return wt(kind, number, ref, ref, sibling)

    def own_copy(number):
        return pltpu.make_async_copy(own_piece(number), piece(dp, number), own_sem.at[number])

    for number in range(3):
        weight_send(0, number).start()
        weight_send(1, 2 - number).start()
    for number in range(3):
        weight_send(3, number).start()
        own_copy(number).start()

    lane = lax.broadcasted_iota(jnp.int32, (NZ, 128), 1)
    named = lane // ROWS * NZ + lax.broadcasted_iota(jnp.int32, (NZ, 128), 0)
    logits = logits_ref[...]
    raised = jnp.exp(logits - jnp.max(logits, axis=0, keepdims=True))
    probs = (raised / jnp.sum(raised, axis=0, keepdims=True)).astype(BF16).astype(F32)
    chosen = jnp.zeros((NZ, 128), F32)
    weight = jnp.zeros((NZ, 128), F32)
    for k in range(TOP):
        same = named == ids_ref[k : k + 1, :]
        chosen += jnp.where(same, 1.0, 0.0)
        weight += jnp.where(same, probs[k : k + 1, :], 0.0)
    chosen = jnp.where(lane % ROWS < live_ref[...], chosen, 0.0)
    row_l = lax.broadcasted_iota(jnp.int32, (128, 128), 0)
    col_l = lax.broadcasted_iota(jnp.int32, (128, 128), 1)
    before = jnp.where((row_l // ROWS == col_l // ROWS) & (row_l < col_l), 1.0, 0.0).astype(BF16)
    rank = jnp.dot(chosen.astype(BF16), before, preferred_element_type=F32)
    slots = jnp.where(chosen > 0.5, rank, -1.0)
    zbuf[z, 0:NZ, D:] = slots.astype(BF16)
    zbuf[z, NZ:, D:] = weight.astype(BF16)

    for h in range(1, 9):
        for side in ring_steps(h):
            wz_arrival(side, h).wait_recv()
            if h < (7 if side == 0 else 8):
                wz_copy(side, h).start()
            wx_copy(0, side, h).start()
            wx_copy(1, side, h).start()
        if h >= 2:
            w_forward(h - 2)
    w_forward(7)
    w_forward(8)
    every = [(side, h) for h in range(9) for side in ring_steps(h)]

    def rs_copy(step, order):
        column = (x + (0, 3, 1, 2)[order]) % NX
        target = (dp + step) % NDP
        at = (step - 1) * 4 + order
        return remote(
            pbuf.at[column, target], rbuf.at[dp, column], rs_send.at[at], rs_recv.at[at], (target, expert)
        )

    def rs_arrival(step, order):
        column = (x + (0, 3, 1, 2)[order]) % NX
        source = (dp + NDP - step) % NDP
        at = (step - 1) * 4 + order
        return remote(
            pbuf.at[column, source], rbuf.at[source, column], rs_send.at[at], rs_recv.at[at], (source, expert)
        )

    for order in range(4):
        column = (x + (0, 3, 1, 2)[order]) % NX
        if order:
            for side, h in every:
                if (order - 1, side) not in ((0, 1), (1, 0)):
                    wx_arrival(order - 1, side, h).wait_recv()
        block = wbuf[pl.ds(column * NZ, NZ)].reshape(FB, FB)
        got = lax.dot_general(attn_ref[...], block, NT, preferred_element_type=F32)
        pbuf[column] = got.astype(BF16).reshape(NDP, ROWS, FB)
        for step in range(1, NDP):
            rs_copy(step, order).start()

    for number in range(3):
        weight_arrival(0, number).wait_recv()
        weight_arrival(1, 2 - number).wait_recv()
        if number == 0:
            weight_send(2, 0).start()
            weight_send(2, 2).start()
        if number == 1:
            weight_send(2, 1).start()
    for number in range(3):
        weight_send(4, number).start()
        weight_send(5, number).start()

    for order in range(4):
        column = (x + (0, 3, 1, 2)[order]) % NX
        for step in range(1, NDP):
            rs_arrival(step, order).wait_recv()
        rbuf[dp, column] = pbuf[column, dp]

    square = jnp.zeros((ROWS, 1), F32)
    for g in range(4):
        cols = slice(g * FB, (g + 1) * FB)
        proj = rbuf[0, g].astype(F32)
        for source in range(1, NDP):
            proj += rbuf[source, g].astype(F32)
        both = (resid_ref[:, cols].astype(F32) + proj).astype(BF16)
        held[:, cols] = both
        wide = both.astype(F32)
        square += jnp.sum(wide * wide, axis=-1, keepdims=True)
    scale = lax.rsqrt(square / D + 1e-06)
    zbuf[z, :, 0:D] = (held[...].astype(F32) * scale * gain_post_ref[...]).astype(BF16)

    def nz_copy(side, h):
        return ring_copy(zbuf.at[z_at(side, h)], side, h, nz_send, nz_recv)

    def nz_arrival(side, h):
        return ring_copy(zbuf.at[z_at(side, h)], side, h - 1, nz_send, nz_recv)

    nz_copy(0, 0).start()
    nz_copy(1, 0).start()

    slot_i = lax.broadcasted_iota(jnp.int32, (64, 128), 0)
    slot_l = lax.broadcasted_iota(jnp.int32, (64, 128), 1)
    slot_k = (slot_i % CAP).astype(F32)
    slot_x = slot_l // ROWS == slot_i // 16
    slot_side = [slot_x & (slot_i // CAP % 2 == side) for side in range(2)]
    fold = jnp.where(
        lax.broadcasted_iota(jnp.int32, (ROWS, 128), 1) % ROWS == lax.broadcasted_iota(jnp.int32, (ROWS, 128), 0), 1.0, 0.0
    ).astype(BF16)
    here = lax.broadcasted_iota(jnp.int32, (NZ, 128), 0) == z

    def table_row(source, begin):
        table = zbuf[source, begin : begin + NZ, D:].astype(F32)
        return jnp.sum(jnp.where(here, table, 0.0), axis=0, keepdims=True)

    def pair_sources(h):
        return (z_at(0, h), z_at(1, h)) if h < PAIRS else (z, z_at(1, h))

    def hits(source, side):
        return slot_side[side] & (table_row(source, 0) == slot_k)

    def compact(h):
        total = jnp.zeros((64, D), F32)
        for side, source in enumerate(pair_sources(h)):
            picked = jnp.where(hits(source, side), 1.0, 0.0).astype(BF16)
            choose = lax.dot_general(picked, fold, NT, preferred_element_type=F32).astype(BF16)
            total += jnp.dot(choose, zbuf[source, :, 0:D], preferred_element_type=F32)
        cbuf[h - 1] = total.astype(BF16).reshape(NX, 16, D)

    def cx_copy(h, step):
        at = (h - 1) * 3 + step - 1
        target = (x + step) % NX
        return remote(cbuf.at[h - 1, target], xbuf.at[h - 1, x], cx_send.at[at], cx_recv.at[at], xpeer[step])

    def cx_arrival(h, step):
        at = (h - 1) * 3 + step - 1
        source = (x + NX - step) % NX
        return remote(
            cbuf.at[h - 1, source], xbuf.at[h - 1, source], cx_send.at[at], cx_recv.at[at], xpeer[NX - step]
        )

    def yx_copy(h, step):
        at = (h - 1) * 3 + step - 1
        target = (x + step) % NX
        return remote(ybuf.at[h - 1, target], ret.at[h - 1, x], yx_send.at[at], yx_recv.at[at], xpeer[step])

    def yx_arrival(h, step):
        at = (h - 1) * 3 + step - 1
        source = (x + NX - step) % NX
        return remote(
            ybuf.at[h - 1, source], ret.at[h - 1, source], yx_send.at[at], yx_recv.at[at], xpeer[NX - step]
        )

    def expert_first(chunk):
        for h in (2 * chunk + 1, 2 * chunk + 2):
            for step in range(1, NX):
                cx_arrival(h, step).wait_recv()

        def columns(n, carry):
            rows_in = xbuf[2 * chunk : 2 * chunk + 2].reshape(128, D)
            begin = pl.multiple_of(n * 256, 256)
            gate = jnp.dot(rows_in, gu[:, pl.ds(begin, 256)], preferred_element_type=F32)
            up = jnp.dot(rows_in, gu[:, pl.ds(FF + begin, 256)], preferred_element_type=F32)
            inner[:, pl.ds(begin, 256)] = (gate / (1.0 + jnp.exp(-gate)) * up).astype(BF16)
            return carry

        lax.fori_loop(0, FF // 256, columns, 0)

    def expert_second(chunk):
        def columns(n, carry):
            begin = pl.multiple_of(n * DN_COLS, DN_COLS)
            out = jnp.dot(inner[...], dn[n], preferred_element_type=F32)
            ybuf[2 * chunk : 2 * chunk + 2, :, :, pl.ds(begin, DN_COLS)] = out.astype(BF16).reshape(2, NX, 16, DN_COLS)
            return carry

        lax.fori_loop(0, NDP, columns, 0)
        for h in (2 * chunk + 2, 2 * chunk + 1):
            for step in (2, 1, 3):
                yx_copy(h, step).start()
            ret[h - 1, x] = ybuf[h - 1, x]

    for h in range(1, PAIRS + 1):
        for side in ring_steps(h):
            nz_arrival(side, h).wait_recv()
            if h < (7 if side == 0 else 8):
                nz_copy(side, h).start()
        compact(h)
        for step in (2, 1, 3):
            cx_copy(h, step).start()
        xbuf[h - 1, x] = cbuf[h - 1, x]
        if h == 1:
            for number in range(3):
                weight_arrival(2, number).wait_recv()
                weight_send(6, number).start()
        if h == 3:
            for kind in (3, 4, 5, 6):
                for number in range(3):
                    weight_arrival(kind, number).wait_recv()
            for number in range(3):
                own_copy(number).wait()
        if h >= 3:
            (expert_first if h % 2 else expert_second)((h - 3) // 2)
    expert_first(3)
    expert_second(3)

    def partial_sum(h, side):
        source = pair_sources(h)[side]
        scaled = jnp.where(hits(source, side), table_row(source, NZ), 0.0).astype(BF16)
        spread = lax.dot_general(fold, scaled, NT, preferred_element_type=F32).astype(BF16)
        return jnp.dot(spread, ret[h - 1].reshape(64, D), preferred_element_type=F32)

    for h in range(1, PAIRS + 1):
        if h == 7:
            continue
        for step in range(1, NX):
            yx_arrival(h, step).wait_recv()
        for side in range(2):
            part[h - 1, side] = partial_sum(h, side)
    def up_copy(t):
        return remote(up_out.at[t], up_in.at[t], up_send.at[t], up_recv.at[t], above)

    def dn_copy(t):
        return remote(dn_out.at[t], dn_in.at[t], dn_send.at[t], dn_recv.at[t], below)

    up_out[0] = part[7, 1].astype(BF16)
    up_copy(0).start()
    for step in range(1, NX):
        yx_arrival(7, step).wait_recv()
    dn_out[0] = partial_sum(7, 1).astype(BF16)
    dn_copy(0).start()
    part[6, 0] = partial_sum(7, 0)
    for t in range(1, 8):
        up_copy(t - 1).wait_recv()
        up_out[t] = (up_in[t - 1].astype(F32) + part[7 - t, 0]).astype(BF16)
        up_copy(t).start()
        if t < 7:
            dn_copy(t - 1).wait_recv()
            dn_out[t] = (dn_in[t - 1].astype(F32) + part[6 - t, 1]).astype(BF16)
            dn_copy(t).start()
    total = held[...].astype(F32) + part[7, 0]
    dn_copy(6).wait_recv()
    total += dn_in[6].astype(F32)
    up_copy(7).wait_recv()
    final = (total + up_in[7].astype(F32)).astype(BF16)
    stream_ref[...] = final
    wide = final.astype(F32)
    scale = lax.rsqrt(jnp.mean(wide * wide, axis=-1, keepdims=True) + 1e-06)
    normed_ref[...] = (wide * scale * gain_final_ref[...]).astype(BF16)

    for side, h in every + [(1, 0)]:
        if h < (7 if side == 0 else 8):
            wz_copy(side, h).wait_send()
            nz_copy(side, h).wait_send()
    for side, h in every:
        for way in range(3):
            wx_copy(way, side, h).wait_send()
    for order in range(4):
        for step in range(1, NDP):
            rs_copy(step, order).wait_send()
    for kind in range(7):
        for number in range(3):
            weight_send(kind, number).wait_send()
    for h in range(1, PAIRS + 1):
        for step in range(1, NX):
            cx_copy(h, step).wait_send()
            yx_copy(h, step).wait_send()
    for t in range(8):
        up_copy(t).wait_send()
        if t < 7:
            dn_copy(t).wait_send()


def block(*args):
    vmem = pl.BlockSpec(memory_space=pltpu.VMEM)
    hbm = pl.BlockSpec(memory_space=pl.ANY)
    dma = pltpu.SemaphoreType.DMA
    return pl.pallas_call(
        kernel,
        out_shape=[jax.ShapeDtypeStruct((ROWS, D), BF16)] * 2,
        in_specs=[vmem] * 7 + [hbm] * 2 + [vmem],
        out_specs=[vmem] * 2,
        scratch_shapes=[
            pltpu.VMEM((NX * NZ, ROWS, FB), BF16),
            pltpu.VMEM((NX, NDP, ROWS, FB), BF16),
            pltpu.VMEM((NDP, NX, ROWS, FB), BF16),
            pltpu.VMEM((ROWS, D), BF16),
            pltpu.VMEM((NZ, ROWS, D + 128), BF16),
            pltpu.VMEM((PAIRS, NX, 16, D), BF16),
            pltpu.VMEM((PAIRS, NX, 16, D), BF16),
            pltpu.VMEM((128, FF), BF16),
            pltpu.VMEM((PAIRS, NX, 16, D), BF16),
            pltpu.VMEM((PAIRS, NX, 16, D), BF16),
            pltpu.VMEM((PAIRS, 2, ROWS, D), F32),
            pltpu.VMEM((8, ROWS, D), BF16),
            pltpu.VMEM((8, ROWS, D), BF16),
            pltpu.VMEM((7, ROWS, D), BF16),
            pltpu.VMEM((7, ROWS, D), BF16),
            pltpu.VMEM((D, 2 * FF), BF16),
            pltpu.VMEM((NDP, FF, DN_COLS), BF16),
            dma((16,)),
            dma((16,)),
            dma((48,)),
            dma((48,)),
            dma((28,)),
            dma((28,)),
            dma((3,)),
            dma((21,)),
            dma((21,)),
            dma((16,)),
            dma((16,)),
            dma((24,)),
            dma((24,)),
            dma((24,)),
            dma((24,)),
            dma((8,)),
            dma((8,)),
            dma((7,)),
            dma((7,)),
        ],
        compiler_params=pltpu.CompilerParams(
            collective_id=0, has_side_effects=True, vmem_limit_bytes=56 << 20
        ),
    )(*args)


def body(
    attn,
    resid,
    w_out,
    gain_post,
    route_ids,
    route_logits,
    live_count,
    w_gate_up,
    w_down,
    gain_final,
):
    ids = jnp.tile(route_ids[0].T, (1, NX))
    logits = jnp.tile(route_logits[0].T, (1, NX))
    live = jnp.broadcast_to(live_count, (1, 128))
    stream_out, normed_out = block(
        attn[0],
        resid[0],
        w_out.T,
        gain_post[None],
        ids,
        logits,
        live,
        w_gate_up[0],
        w_down[0],
        gain_final[None],
    )
    return (stream_out[None], normed_out[None])


def solution(mesh):
    placed = (
        P("expert", None, "dp"),
        P("expert", "dp", None),
        P("dp", "expert"),
        P(),
        P("expert", "dp", None),
        P("expert", "dp", None),
        P("expert", "dp"),
        P("expert", "dp", None),
        P("expert", None, "dp"),
        P(),
    )
    return jax.shard_map(
        body,
        mesh=mesh,
        in_specs=placed,
        out_specs=(P("expert", "dp", None), P("expert", "dp", None)),
        check_vma=False,
    )
```

```python
import jax
import jax.numpy as jnp
from jax import lax
from jax.experimental import pallas as pl
from jax.experimental.pallas import tpu as pltpu
from jax.sharding import PartitionSpec as P

NX, NZ, NY, NC = 4, 16, 4, 2
NDP = NY * NC
ROWS, D, FB, FF, TOP, CAP = 32, 2048, 512, 768, 8, 8
GU_ROWS, DN_COLS, CUT = D // NDP, D // NDP, 192
PAIRS = NZ // 2
MESH = pl.DeviceIdType.MESH
F32, BF16 = jnp.float32, jnp.bfloat16
NT = (((1,), (1,)), ((), ()))


def remote(src, dst, send_sem, recv_sem, peer):
    return pltpu.make_async_remote_copy(
        src_ref=src,
        dst_ref=dst,
        send_sem=send_sem,
        recv_sem=recv_sem,
        device_id=peer,
        device_id_type=MESH,
    )


def kernel(
    attn_ref,
    resid_ref,
    w_ref,
    gain_post_ref,
    ids_ref,
    logits_ref,
    live_ref,
    gate_up_ref,
    down_ref,
    gain_final_ref,
    stream_ref,
    normed_ref,
    abuf,
    resid,
    wbuf,
    pbuf,
    rbuf,
    sums_out,
    sums_in,
    sums,
    held,
    zbuf,
    cbuf,
    xbuf,
    cmat,
    inner,
    ybuf,
    ret,
    part,
    up_out,
    up_in,
    dn_out,
    dn_in,
    gu,
    dn,
    own_sem,
    sent,
    w_recv,
    a_recv,
    rs_recv,
    sx_recv,
    near_recv,
    far_recv,
    sib_recv,
    nz_recv,
    cx_recv,
    yx_recv,
    up_recv,
    dn_recv,
):
    dp = lax.axis_index("dp")
    expert = lax.axis_index("expert")
    x, z = expert // NZ, expert % NZ
    y, core = dp // NC, dp % NC
    zpeer = {step: (dp, x * NZ + (z + NZ + step) % NZ) for step in (-2, -1, 1, 2)}
    above, below = zpeer[1], zpeer[-1]

    def xpeer(step):
        return (dp, (x + step) % NX * NZ + z)

    right, left = xpeer(1), xpeer(3)
    y_up, y_down = ((y + 1) % NY * NC + core, expert), ((y + NY - 1) % NY * NC + core, expert)
    sibling = (y * NC + 1 - core, expert)

    W, A, RS, SX, GU, DN, NZS, CX, YX, UP, DOWN = range(11)

    def left_all(kind, ref):
        remote(ref, ref, sent.at[kind], rs_recv.at[0], right).wait_send()

    def arrived(ref, semaphore):
        remote(ref, ref, sent.at[0], semaphore, right).wait_recv()

    def local(src, dst, at):
        return pltpu.make_async_copy(src, dst, own_sem.at[at])

    attn_in = local(attn_ref, abuf.at[x], 3)
    resid_in = local(resid_ref, resid, 4)
    attn_in.start()
    resid_in.start()
    same = lax.broadcasted_iota(jnp.int32, (ROWS, ROWS), 0) == lax.broadcasted_iota(jnp.int32, (ROWS, ROWS), 1)
    eye = jnp.where(same, 1.0, 0.0).astype(BF16)
    wbuf[z] = lax.dot_general(eye, w_ref[...], NT, preferred_element_type=F32).astype(BF16)

    peers = list(zpeer.values()) + [xpeer(step) for step in range(1, NX)]
    peers += [((dp + step) % NDP, expert) for step in range(1, NDP)]
    barrier = pltpu.get_barrier_semaphore()
    for peer in peers:
        pl.semaphore_signal(barrier, inc=1, device_id=peer, device_id_type=MESH)
    pl.semaphore_wait(barrier, len(peers))

    def z_at(side, h):
        return (z + (h if side == 0 else NZ - h)) % NZ

    def w_copy(side, h):
        ref = wbuf.at[z_at(side, max(h - 2, 0))]
        step = (1 if side else -1) * min(h, 2)
        return remote(ref, ref, sent.at[W], w_recv.at[side * 8 + h - 1], zpeer[step])

    def half_rows(half):
        return pl.ds(half * 128, 128)

    def a_copy(way, half):
        if way < 2:
            src, dst = attn_ref.at[half_rows(half)], abuf.at[x, half_rows(half)]
        else:
            src = dst = abuf.at[(x + (3, 1)[half]) % NX, half_rows(half)]
        peer = (right, left)[way if way < 2 else half]
        return remote(src, dst, sent.at[A], a_recv.at[way * 2 + half], peer)

    def a_arrived(way, half):
        arrived(abuf.at[(x + (3, 1, 2)[way]) % NX, half_rows(half)], a_recv.at[way * 2 + half])

    for h in (1, 2):
        w_copy(1, h).start()
        w_copy(0, h).start()
    for half in range(2):
        a_copy(0, half).start()
        a_copy(1, 1 - half).start()

    def piece(owner, number):
        if number == 2:
            return dn.at[owner]
        begin = pl.multiple_of(owner * GU_ROWS, GU_ROWS)
        return gu.at[pl.ds(begin, CUT)] if number == 0 else gu.at[pl.ds(begin + CUT, GU_ROWS - CUT)]

    def own_piece(number):
        if number == 2:
            return down_ref
        return gate_up_ref.at[pl.ds(0, CUT)] if number == 0 else gate_up_ref.at[pl.ds(CUT, GU_ROWS - CUT)]

    def owner_of(step, on_core):
        return (y + step) % NY * NC + on_core

    def weight_copy(src, dst, number, recv, peer):
        return remote(src, dst, sent.at[DN if number == 2 else GU], recv, peer)

    def to_near(side, number):
        peer = (y_up, y_down)[side]
        return weight_copy(own_piece(number), piece(dp, number), number, near_recv.at[side * 3 + number], peer)

    def near_arrived(side, number):
        arrived(piece(owner_of((3, 1)[side], core), number), near_recv.at[side * 3 + number])

    def to_far(number):
        ref = piece(owner_of(3 if number == 0 else 1, core), number)
        return weight_copy(ref, ref, number, far_recv.at[number], y_up if number == 0 else y_down)

    def to_sibling(step, number):
        recv = sib_recv.at[1 if number == 2 else 0]
        owner = owner_of(step, core)
        src = piece(owner, number) if step else own_piece(number)
        return weight_copy(src, piece(owner, number), number, recv, sibling)

    def own_copy(number):
        return local(own_piece(number), piece(dp, number), number)

    for number in range(3):
        to_near(0, number).start()
        to_near(1, 2 - number).start()
    for number in range(3):
        to_sibling(0, number).start()
        own_copy(number).start()

    logits = logits_ref[...]
    raised = jnp.exp(logits - jnp.max(logits, axis=1, keepdims=True))
    probs = (raised / jnp.sum(raised, axis=1, keepdims=True)).astype(BF16)
    fold = jnp.where(
        lax.broadcasted_iota(jnp.int32, (ROWS, 128), 1) % ROWS == lax.broadcasted_iota(jnp.int32, (ROWS, 128), 0), 1.0, 0.0
    ).astype(BF16)
    ids = ids_ref[...].astype(F32).astype(BF16)
    ids_t = lax.dot_general(ids, fold, (((0,), (0,)), ((), ())), preferred_element_type=F32)
    probs_t = lax.dot_general(probs, fold, (((0,), (0,)), ((), ())), preferred_element_type=F32)
    lane = lax.broadcasted_iota(jnp.int32, (NZ, 128), 1)
    named = (lane // ROWS * NZ + lax.broadcasted_iota(jnp.int32, (NZ, 128), 0)).astype(F32)
    chosen = jnp.zeros((NZ, 128), F32)
    weight = jnp.zeros((NZ, 128), F32)
    for k in range(TOP):
        found = named == ids_t[k : k + 1, :]
        chosen += jnp.where(found, 1.0, 0.0)
        weight += jnp.where(found, probs_t[k : k + 1, :], 0.0)
    chosen = jnp.where(lane % ROWS < live_ref[...], chosen, 0.0)
    row_l = lax.broadcasted_iota(jnp.int32, (128, 128), 0)
    col_l = lax.broadcasted_iota(jnp.int32, (128, 128), 1)
    before = jnp.where((row_l // ROWS == col_l // ROWS) & (row_l < col_l), 1.0, 0.0).astype(BF16)
    rank = jnp.dot(chosen.astype(BF16), before, preferred_element_type=F32)
    zbuf[z, 0, :, D:] = jnp.where(chosen > 0.5, rank, -1.0).astype(BF16)
    zbuf[z, 1, :, D:] = weight.astype(BF16)

    for h in range(1, 9):
        for side in (1, 0):
            if h <= 7 + side:
                arrived(wbuf.at[z_at(side, h)], w_recv.at[side * 8 + h - 1])
                if h + 2 <= 7 + side:
                    w_copy(side, h + 2).start()
        if h == 2:
            a_arrived(0, 0)
            a_copy(2, 0).start()
            a_arrived(1, 1)
            a_copy(2, 1).start()
    attn_in.wait()
    resid_in.wait()
    for way, half in ((0, 1), (1, 0), (2, 0), (2, 1)):
        a_arrived(way, half)

    def product(order, carry):
        got = lax.dot_general(
            abuf[(x + 3 - order) % NX], wbuf[...].reshape(FB, FB), NT, preferred_element_type=F32
        )
        pbuf[:, order] = got.astype(BF16).reshape(NDP, ROWS, FB)

        @pl.when(order % 2 == 1)
        def _():
            pair = pl.ds(order - 1, 2)
            for step in (4, 3, 5, 2, 6, 1, 7):
                target = (dp + step) % NDP
                remote(
                    pbuf.at[target, pair], rbuf.at[dp, pair], sent.at[RS], rs_recv.at[order // 2], (target, expert)
                ).start()

        return carry

    lax.fori_loop(0, NX, product, 0)

    def sum_up(order, carry):
        @pl.when(order % 2 == 0)
        def _():
            arrived(rbuf.at[pl.ds(0, 7), pl.ds(0, 2)], rs_recv.at[order // 2])

        total = pbuf[dp, order].astype(F32)
        for step in range(1, NDP):
            total += rbuf[(dp + step) % NDP, order].astype(F32)

        @pl.when(order < 3)
        def _():
            sums_out[order] = total.astype(BF16)
            remote(sums_out.at[order], sums_in.at[x], sent.at[SX], sx_recv.at[0], xpeer(3 - order)).start()

        @pl.when(order == 3)
        def _():
            sums[x] = total

        return carry

    lax.fori_loop(0, NX, sum_up, 0)

    for number in range(3):
        near_arrived(0, number)
        near_arrived(1, 2 - number)
        if number == 0:
            to_far(0).start()
            to_far(2).start()
        if number == 1:
            to_far(1).start()
    for number in range(3):
        to_sibling(3, number).start()
        to_sibling(1, number).start()

    arrived(sums_in.at[pl.ds(0, 3)], sx_recv.at[0])
    for step in range(1, NX):
        source = (x + step) % NX
        sums[source] = sums_in[source].astype(F32)

    square = jnp.zeros((ROWS, 1), F32)
    for g in range(4):
        cols = slice(g * FB, (g + 1) * FB)
        both = (resid[:, cols].astype(F32) + sums[g]).astype(BF16)
        held[:, cols] = both
        wide = both.astype(F32)
        square += jnp.sum(wide * wide, axis=-1, keepdims=True)
    scale = lax.rsqrt(square / D + 1e-06)
    normed = (held[...].astype(F32) * scale * gain_post_ref[...]).astype(BF16)
    zbuf[z, :, :, 0:D] = normed.reshape(2, 16, D)

    def nz_copy(side, h, half):
        ref = zbuf.at[z_at(side, h), half]
        return remote(ref, ref, sent.at[NZS], nz_recv.at[(side * 8 + h) * 2 + half], above if side else below)

    for half in range(2):
        nz_copy(1, 0, half).start()
        nz_copy(0, 0, half).start()

    slot_i = lax.broadcasted_iota(jnp.int32, (64, 128), 0)
    slot_l = lax.broadcasted_iota(jnp.int32, (64, 128), 1)
    slot_k = (slot_i % CAP).astype(F32)
    slot_x = slot_l // ROWS == slot_i // 16
    slot_side = [slot_x & (slot_i // CAP % 2 == side) for side in range(2)]
    here = lax.broadcasted_iota(jnp.int32, (NZ, 128), 0) == z

    def table_row(source, half):
        table = zbuf[source, half, :, D:].astype(F32)
        return jnp.sum(jnp.where(here, table, 0.0), axis=0, keepdims=True)

    def compact(h):
        total = jnp.zeros((64, D), F32)
        for side, source in enumerate((z_at(0, h % PAIRS), z_at(1, h))):
            hit = slot_side[side] & (table_row(source, 0) == slot_k)
            picked = jnp.where(hit, 1.0, 0.0).astype(BF16)
            choose = lax.dot_general(picked, fold, NT, preferred_element_type=F32).astype(BF16)
            scaled = jnp.where(hit, table_row(source, 1), 0.0).astype(BF16)
            spread = lax.dot_general(fold, scaled, NT, preferred_element_type=F32)
            cmat[h - 1, side * ROWS : (side + 1) * ROWS] = spread.astype(BF16)
            total += jnp.dot(choose, zbuf[source, :, :, 0:D].reshape(ROWS, D), preferred_element_type=F32)
        cbuf[h - 1] = total.astype(BF16).reshape(NX, 16, D)
        for step in (2, 1, 3):
            target = (x + step) % NX
            remote(
                cbuf.at[h - 1, target], xbuf.at[h - 1, x], sent.at[CX], cx_recv.at[h - 1], xpeer(step)
            ).start()
        xbuf[h - 1, x] = cbuf[h - 1, x]

    def ring_step(h, carry):
        for half in range(2):
            for side in (1, 0):

                @pl.when(h <= 7 + side)
                def _():
                    arrived(zbuf.at[z_at(side, h), half], nz_recv.at[(side * 8 + h - 1) * 2 + half])

                @pl.when(h < 7 + side)
                def _():
                    nz_copy(side, h, half).start()


        @pl.when(h == 7)
        def _():
            for number in range(3):
                arrived(piece(owner_of(2, core), number), far_recv.at[number])
                to_sibling(2, number).start()

        compact(h)
        return carry

    lax.fori_loop(1, PAIRS + 1, ring_step, 0)

    arrived(gu.at[pl.ds(0, 4 * GU_ROWS)], sib_recv.at[0])
    arrived(dn.at[pl.ds(0, 4)], sib_recv.at[1])
    for number in range(3):
        own_copy(number).wait()

    def chunk_step(order, carry):
        begin = (1 - order) * 4
        for pair in range(4):
            arrived(xbuf.at[begin + pair, pl.ds(0, 3)], cx_recv.at[begin + pair])

        def hidden(n, carry):
            rows_in = xbuf[pl.ds(begin, 4)].reshape(256, D)
            at = pl.multiple_of(n * 256, 256)
            gate = jnp.dot(rows_in, gu[:, pl.ds(at, 256)], preferred_element_type=F32)
            up = jnp.dot(rows_in, gu[:, pl.ds(FF + at, 256)], preferred_element_type=F32)
            inner[:, pl.ds(at, 256)] = (gate / (1.0 + jnp.exp(-gate)) * up).astype(BF16)
            return carry

        lax.fori_loop(0, FF // 256, hidden, 0)

        def outer(n, carry):
            out = jnp.dot(inner[...], dn[n], preferred_element_type=F32)
            at = pl.multiple_of(n * DN_COLS, DN_COLS)
            ybuf[pl.ds(begin, 4), :, :, pl.ds(at, DN_COLS)] = out.astype(BF16).reshape(4, NX, 16, DN_COLS)
            return carry

        lax.fori_loop(0, NDP, outer, 0, unroll=2)
        for pair in range(3, -1, -1):
            for step in (2, 1, 3):
                target = (x + step) % NX
                remote(
                    ybuf.at[begin + pair, target],
                    ret.at[begin + pair, x],
                    sent.at[YX],
                    yx_recv.at[begin + pair],
                    xpeer(step),
                ).start()
            ret[begin + pair, x] = ybuf[begin + pair, x]
        return carry

    lax.fori_loop(0, 2, chunk_step, 0)

    def up_copy(t, half):
        return remote(up_out.at[t, half], up_in.at[t, half], sent.at[UP], up_recv.at[2 * t + half], above)

    def dn_copy(t, half):
        return remote(dn_out.at[t, half], dn_in.at[t, half], sent.at[DOWN], dn_recv.at[2 * t + half], below)

    def keep(pair):
        arrived(ret.at[pair, pl.ds(0, 3)], yx_recv.at[pair])
        both = jnp.dot(cmat[pair], ret[pair].reshape(64, D), preferred_element_type=F32)
        part[pair] = both.reshape(2, 2, 16, D)

    def reduce_step(t, carry):
        @pl.when(t == 0)
        def _():
            keep(7)

        for half in range(2):
            total = part[7 - t, (8 - t) // 8, half]
            up_out[t, half] = total.astype(BF16)

            @pl.when(t > 0)
            def _():
                arrived(up_in.at[t - 1, half], up_recv.at[2 * (t - 1) + half])
                up_out[t, half] = (up_in[t - 1, half].astype(F32) + total).astype(BF16)

            up_copy(t, half).start()

        @pl.when(t < 7)
        def _():
            keep(6 - t)
            for half in range(2):
                total = part[6 - t, 1, half]
                dn_out[t, half] = total.astype(BF16)

                @pl.when(t > 0)
                def _():
                    arrived(dn_in.at[t - 1, half], dn_recv.at[2 * (t - 1) + half])
                    dn_out[t, half] = (dn_in[t - 1, half].astype(F32) + total).astype(BF16)

                dn_copy(t, half).start()

        return carry

    lax.fori_loop(0, 8, reduce_step, 0)
    for half in range(2):
        rows = slice(half * 16, half * 16 + 16)
        total = held[rows].astype(F32) + part[7, 0, half]
        arrived(dn_in.at[6, half], dn_recv.at[12 + half])
        total += dn_in[6, half].astype(F32)
        arrived(up_in.at[7, half], up_recv.at[14 + half])
        final = (total + up_in[7, half].astype(F32)).astype(BF16)
        stream_ref[rows] = final
        wide = final.astype(F32)
        scale = lax.rsqrt(jnp.mean(wide * wide, axis=-1, keepdims=True) + 1e-06)
        normed_ref[rows] = (wide * scale * gain_final_ref[...]).astype(BF16)

    left_all(W, wbuf.at[pl.ds(0, 15)])
    left_all(A, abuf.at[pl.ds(0, 3)])
    left_all(RS, rbuf.at[pl.ds(0, 7)])
    left_all(SX, sums_out)
    left_all(GU, gu.at[pl.ds(0, 7 * GU_ROWS)])
    left_all(DN, dn.at[pl.ds(0, 7)])
    left_all(NZS, zbuf.at[pl.ds(0, 15)])
    left_all(CX, cbuf.at[pl.ds(0, 6)])
    left_all(YX, ybuf.at[pl.ds(0, 6)])
    left_all(UP, up_out)
    left_all(DOWN, dn_out)


def block(*args):
    vmem = pl.BlockSpec(memory_space=pltpu.VMEM)
    hbm = pl.BlockSpec(memory_space=pl.ANY)
    dma = pltpu.SemaphoreType.DMA
    counts = (5, 11, 16, 6, 2, 1, 6, 3, 2, 32, 8, 8, 16, 14)
    return pl.pallas_call(
        kernel,
        out_shape=[jax.ShapeDtypeStruct((ROWS, D), BF16)] * 2,
        in_specs=[hbm] * 2 + [vmem] * 5 + [hbm] * 2 + [vmem],
        out_specs=[vmem] * 2,
        scratch_shapes=[
            pltpu.VMEM((NX, NDP * ROWS, FB), BF16),
            pltpu.VMEM((ROWS, D), BF16),
            pltpu.VMEM((NZ, ROWS, FB), BF16),
            pltpu.VMEM((NDP, NX, ROWS, FB), BF16),
            pltpu.VMEM((NDP, NX, ROWS, FB), BF16),
            pltpu.VMEM((3, ROWS, FB), BF16),
            pltpu.VMEM((NX, ROWS, FB), BF16),
            pltpu.VMEM((NX, ROWS, FB), F32),
            pltpu.VMEM((ROWS, D), BF16),
            pltpu.VMEM((NZ, 2, 16, D + 128), BF16),
            pltpu.VMEM((PAIRS, NX, 16, D), BF16),
            pltpu.VMEM((PAIRS, NX, 16, D), BF16),
            pltpu.VMEM((PAIRS, 64, 64), BF16),
            pltpu.VMEM((256, FF), BF16),
            pltpu.VMEM((PAIRS, NX, 16, D), BF16),
            pltpu.VMEM((PAIRS, NX, 16, D), BF16),
            pltpu.VMEM((PAIRS, 2, 2, 16, D), F32),
            pltpu.VMEM((8, 2, 16, D), BF16),
            pltpu.VMEM((8, 2, 16, D), BF16),
            pltpu.VMEM((7, 2, 16, D), BF16),
            pltpu.VMEM((7, 2, 16, D), BF16),
            pltpu.VMEM((D, 2 * FF), BF16),
            pltpu.VMEM((NDP, FF, DN_COLS), BF16),
        ]
        + [dma((count,)) for count in counts],
        compiler_params=pltpu.CompilerParams(
            collective_id=0, has_side_effects=True, vmem_limit_bytes=56 << 20
        ),
    )(*args)


def body(
    attn,
    resid,
    w_out,
    gain_post,
    route_ids,
    route_logits,
    live_count,
    w_gate_up,
    w_down,
    gain_final,
):
    stream_out, normed_out = block(
        attn[0],
        resid[0],
        w_out,
        gain_post[None],
        route_ids[0],
        route_logits[0],
        live_count,
        w_gate_up[0],
        w_down[0],
        gain_final[None],
    )
    return (stream_out[None], normed_out[None])


def solution(mesh):
    placed = (
        P("expert", None, "dp"),
        P("expert", "dp", None),
        P("dp", "expert"),
        P(),
        P("expert", "dp", None),
        P("expert", "dp", None),
        P("expert", "dp"),
        P("expert", "dp", None),
        P("expert", None, "dp"),
        P(),
    )
    return jax.shard_map(
        body,
        mesh=mesh,
        in_specs=placed,
        out_specs=(P("expert", "dp", None), P("expert", "dp", None)),
        check_vma=False,
    )
```

```python
import jax
import jax.numpy as jnp
from jax import lax
from jax.experimental import pallas as pl
from jax.experimental.pallas import tpu as pltpu
from jax.sharding import PartitionSpec as P

NX, NZ, NY, NC = 4, 16, 4, 2
NDP = NY * NC
ROWS, D, FB, FF, TOP, CAP = 32, 2048, 512, 768, 8, 8
GU_ROWS, DN_COLS, CUT = D // NDP, D // NDP, 192
PAIRS = NZ // 2
MESH = pl.DeviceIdType.MESH
F32, BF16 = jnp.float32, jnp.bfloat16
NT = (((1,), (1,)), ((), ()))


def remote(src, dst, send_sem, recv_sem, peer):
    return pltpu.make_async_remote_copy(
        src_ref=src,
        dst_ref=dst,
        send_sem=send_sem,
        recv_sem=recv_sem,
        device_id=peer,
        device_id_type=MESH,
    )


def kernel(
    attn_ref,
    resid_ref,
    w_ref,
    gain_post_ref,
    ids_ref,
    logits_ref,
    live_ref,
    gate_up_ref,
    down_ref,
    gain_final_ref,
    stream_ref,
    normed_ref,
    abuf,
    resid,
    wbuf,
    pbuf,
    qbuf,
    sbuf,
    rbuf,
    sums_out,
    sums_in,
    sums,
    held,
    zbuf,
    cbuf,
    xbuf,
    cmat,
    inner,
    ybuf,
    ret,
    part,
    rs_out,
    rs_in,
    gu,
    dn,
    own_sem,
    sent,
    w_recv,
    a_recv,
    pair_recv,
    rs_recv,
    sx_recv,
    near_recv,
    far_recv,
    sib_recv,
    nz_recv,
    cx_recv,
    yx_recv,
    ring_recv,
):
    dp = lax.axis_index("dp")
    expert = lax.axis_index("expert")
    x, z = expert // NZ, expert % NZ
    y, core = dp // NC, dp % NC
    zpeer = {step: (dp, x * NZ + (z + NZ + step) % NZ) for step in (-6, -3, -2, -1, 1, 2, 3, 6)}
    above, below = zpeer[1], zpeer[-1]

    def xpeer(step):
        return (dp, (x + step) % NX * NZ + z)

    right, left = xpeer(1), xpeer(3)

    def ypeer(step):
        return ((y + step) % NY * NC + core, expert)

    y_up, y_down = ypeer(1), ypeer(3)
    sibling = (y * NC + 1 - core, expert)

    W, A, PAIR, RS, SX, GU, DN, NZS, CX, YX, UP = range(11)

    def left_all(kind, ref):
        remote(ref, ref, sent.at[kind], rs_recv.at[0], right).wait_send()

    def arrived(ref, semaphore):
        remote(ref, ref, sent.at[0], semaphore, right).wait_recv()

    def local(src, dst, at):
        return pltpu.make_async_copy(src, dst, own_sem.at[at])

    attn_in = local(attn_ref, abuf.at[x], 3)
    resid_in = local(resid_ref, resid, 4)
    attn_in.start()
    resid_in.start()
    wbuf[z] = w_ref[...]

    peers = list(zpeer.values()) + [xpeer(step) for step in range(1, NX)]
    peers += [ypeer(step) for step in range(1, NY)] + [sibling]
    barrier = pltpu.get_barrier_semaphore()
    for peer in peers:
        pl.semaphore_signal(barrier, inc=1, device_id=peer, device_id_type=MESH)
    pl.semaphore_wait(barrier, len(peers))

    def z_at(side, h):
        return (z + (h if side == 0 else NZ - h)) % NZ

    jumps = {6: 6, 3: 3, 1: 1, 8: 2, 7: 1, 5: 2, 4: 1, 2: 1}

    def w_copy(side, h):
        ref = wbuf.at[z_at(side, h - jumps[h])]
        return remote(ref, ref, sent.at[W], w_recv.at[side * 8 + h - 1], zpeer[jumps[h] if side else -jumps[h]])

    def half_rows(half):
        return pl.ds(half * 128, 128)

    def a_copy(way, half):
        if way < 2:
            src, dst = attn_ref.at[half_rows(half)], abuf.at[x, half_rows(half)]
        else:
            src = dst = abuf.at[(x + (3, 1)[half]) % NX, half_rows(half)]
        peer = (right, left)[way if way < 2 else half]
        return remote(src, dst, sent.at[A], a_recv.at[way * 2 + half], peer)

    def a_arrived(way, half):
        arrived(abuf.at[(x + (3, 1, 2)[way]) % NX, half_rows(half)], a_recv.at[way * 2 + half])

    for h in (6, 3, 1):
        w_copy(1, h).start()
        w_copy(0, h).start()
    for half in range(2):
        a_copy(0, half).start()
        a_copy(1, 1 - half).start()

    def piece(owner, number):
        if number == 2:
            return dn.at[owner]
        begin = pl.multiple_of(owner * GU_ROWS, GU_ROWS)
        return gu.at[pl.ds(begin, CUT)] if number == 0 else gu.at[pl.ds(begin + CUT, GU_ROWS - CUT)]

    def own_piece(number):
        if number == 2:
            return down_ref
        return gate_up_ref.at[pl.ds(0, CUT)] if number == 0 else gate_up_ref.at[pl.ds(CUT, GU_ROWS - CUT)]

    def owner_of(step, on_core):
        return (y + step) % NY * NC + on_core

    def weight_copy(src, dst, number, recv, peer):
        return remote(src, dst, sent.at[DN if number == 2 else GU], recv, peer)

    def to_near(side, number):
        peer = (y_up, y_down)[side]
        return weight_copy(own_piece(number), piece(dp, number), number, near_recv.at[side * 3 + number], peer)

    def near_arrived(side, number):
        arrived(piece(owner_of((3, 1)[side], core), number), near_recv.at[side * 3 + number])

    def to_far(number):
        ref = piece(owner_of(3 if number == 0 else 1, core), number)
        return weight_copy(ref, ref, number, far_recv.at[number], y_up if number == 0 else y_down)

    def to_sibling(step, number):
        recv = sib_recv.at[1 if number == 2 else 0]
        owner = owner_of(step, core)
        src = piece(owner, number) if step else own_piece(number)
        return weight_copy(src, piece(owner, number), number, recv, sibling)

    def own_copy(number):
        return local(own_piece(number), piece(dp, number), number)

    for number in range(3):
        to_near(0, number).start()
        to_near(1, 2 - number).start()
    for number in range(3):
        to_sibling(0, number).start()
        own_copy(number).start()

    logits = logits_ref[...]
    raised = jnp.exp(logits - jnp.max(logits, axis=0, keepdims=True))
    probs = (raised / jnp.sum(raised, axis=0, keepdims=True)).astype(BF16)
    fold = jnp.where(
        lax.broadcasted_iota(jnp.int32, (ROWS, 128), 1) % ROWS == lax.broadcasted_iota(jnp.int32, (ROWS, 128), 0), 1.0, 0.0
    ).astype(BF16)
    ids = ids_ref[...].astype(F32).astype(BF16)
    ids_t = jnp.dot(ids, fold, preferred_element_type=F32)
    probs_t = jnp.dot(probs, fold, preferred_element_type=F32)
    lane = lax.broadcasted_iota(jnp.int32, (NZ, 128), 1)
    named = (lane // ROWS * NZ + lax.broadcasted_iota(jnp.int32, (NZ, 128), 0)).astype(F32)
    chosen = jnp.zeros((NZ, 128), F32)
    weight = jnp.zeros((NZ, 128), F32)
    for k in range(TOP):
        found = named == ids_t[k : k + 1, :]
        chosen += jnp.where(found, 1.0, 0.0)
        weight += jnp.where(found, probs_t[k : k + 1, :], 0.0)
    chosen = jnp.where(lane % ROWS < live_ref[...], chosen, 0.0)
    row_l = lax.broadcasted_iota(jnp.int32, (128, 128), 0)
    col_l = lax.broadcasted_iota(jnp.int32, (128, 128), 1)
    before = jnp.where((row_l // ROWS == col_l // ROWS) & (row_l < col_l), 1.0, 0.0).astype(BF16)
    rank = jnp.dot(chosen.astype(BF16), before, preferred_element_type=F32)
    zbuf[z, 0:NZ, D:] = jnp.where(chosen > 0.5, rank, -1.0).astype(BF16)
    zbuf[z, NZ:, D:] = weight.astype(BF16)

    for h, onwards in ((1, (2,)), (3, (5, 4)), (6, (8, 7))):
        for side in (1, 0):
            arrived(wbuf.at[z_at(side, h)], w_recv.at[side * 8 + h - 1])
            for far in onwards:
                if far <= 7 + side:
                    w_copy(side, far).start()
        if h == 3:
            a_arrived(0, 0)
            a_copy(2, 0).start()
            a_arrived(1, 1)
            a_copy(2, 1).start()
    for h in (2, 4, 5, 7, 8):
        for side in (1, 0):
            if h <= 7 + side:
                arrived(wbuf.at[z_at(side, h)], w_recv.at[side * 8 + h - 1])
    attn_in.wait()
    resid_in.wait()
    for way, half in ((0, 1), (1, 0), (2, 0), (2, 1)):
        a_arrived(way, half)

    def product(order, carry):
        got = lax.dot_general(
            abuf[(x + 3 - order) % NX], wbuf[...].reshape(FB, FB), NT, preferred_element_type=F32
        )
        blocks = got.astype(BF16).reshape(NY, NC, ROWS, FB)
        for half in range(NC):
            pbuf[half, :, order] = blocks[:, half]
        remote(
            pbuf.at[1 - core, :, order], qbuf.at[:, order], sent.at[PAIR], pair_recv.at[order], sibling
        ).start()
        return carry

    lax.fori_loop(0, NX, product, 0)

    def exchange(order, carry):
        arrived(qbuf.at[:, order], pair_recv.at[order])
        sbuf[:, order] = (pbuf[core, :, order].astype(F32) + qbuf[:, order].astype(F32)).astype(BF16)
        for step in (2, 1, 3):
            target = (y + step) % NY
            remote(
                sbuf.at[target, order], rbuf.at[y, order], sent.at[RS], rs_recv.at[order], ypeer(step)
            ).start()
        return carry

    lax.fori_loop(0, NX, exchange, 0)

    def sum_up(order, carry):
        arrived(rbuf.at[pl.ds(0, 3), order], rs_recv.at[order])
        total = pbuf[core, y, order].astype(F32) + qbuf[y, order].astype(F32)
        for step in range(1, NY):
            total += rbuf[(y + step) % NY, order].astype(F32)

        @pl.when(order < 3)
        def _():
            sums_out[order] = total.astype(BF16)
            remote(sums_out.at[order], sums_in.at[x], sent.at[SX], sx_recv.at[0], xpeer(3 - order)).start()

        @pl.when(order == 3)
        def _():
            sums[x] = total

        return carry

    lax.fori_loop(0, NX, sum_up, 0)

    for number in range(3):
        near_arrived(0, number)
        near_arrived(1, 2 - number)
        if number == 0:
            to_far(0).start()
            to_far(2).start()
        if number == 1:
            to_far(1).start()
    for number in range(3):
        to_sibling(3, number).start()
        to_sibling(1, number).start()

    arrived(sums_in.at[pl.ds(0, 3)], sx_recv.at[0])
    for step in range(1, NX):
        source = (x + step) % NX
        sums[source] = sums_in[source].astype(F32)

    square = jnp.zeros((ROWS, 1), F32)
    for g in range(4):
        cols = slice(g * FB, (g + 1) * FB)
        both = (resid[:, cols].astype(F32) + sums[g]).astype(BF16)
        held[:, cols] = both
        wide = both.astype(F32)
        square += jnp.sum(wide * wide, axis=-1, keepdims=True)
    scale = lax.rsqrt(square / D + 1e-06)
    normed = (held[...].astype(F32) * scale * gain_post_ref[...]).astype(BF16)
    zbuf[z, :, 0:D] = normed

    def row_chunk(side, h, c):
        return zbuf.at[z_at(side, h), :, pl.ds(c * FB, FB if c < 3 else FB + 128)]

    def nz_copy(side, h, c):
        ref = row_chunk(side, h, c)
        return remote(ref, ref, sent.at[NZS], nz_recv.at[(side * 8 + h) * 4 + c], above if side else below)

    for c in range(4):
        nz_copy(1, 0, c).start()
        nz_copy(0, 0, c).start()

    slot_i = lax.broadcasted_iota(jnp.int32, (64, 128), 0)
    slot_l = lax.broadcasted_iota(jnp.int32, (64, 128), 1)
    slot_k = (slot_i % CAP).astype(F32)
    slot_x = slot_l // ROWS == slot_i // 16
    slot_side = [slot_x & (slot_i // CAP % 2 == side) for side in range(2)]
    here = lax.broadcasted_iota(jnp.int32, (NZ, 128), 0) == z

    def table_row(source, half):
        table = zbuf[source, half * NZ : (half + 1) * NZ, D:].astype(F32)
        return jnp.sum(jnp.where(here, table, 0.0), axis=0, keepdims=True)

    def compact(h):
        total = jnp.zeros((64, D), F32)
        for side, source in enumerate((z_at(0, h % PAIRS), z_at(1, h))):
            hit = slot_side[side] & (table_row(source, 0) == slot_k)
            picked = jnp.where(hit, 1.0, 0.0).astype(BF16)
            choose = lax.dot_general(picked, fold, NT, preferred_element_type=F32).astype(BF16)
            scaled = jnp.where(hit, table_row(source, 1), 0.0).astype(BF16)
            spread = lax.dot_general(fold, scaled, NT, preferred_element_type=F32)
            cmat[h - 1, side * ROWS : (side + 1) * ROWS] = spread.astype(BF16)
            total += jnp.dot(choose, zbuf[source, :, 0:D], preferred_element_type=F32)
        cbuf[h - 1] = total.astype(BF16).reshape(NX, 16, D)
        for step in (2, 1, 3):
            target = (x + step) % NX
            remote(
                cbuf.at[h - 1, target], xbuf.at[h - 1, x], sent.at[CX], cx_recv.at[h - 1], xpeer(step)
            ).start()
        xbuf[h - 1, x] = cbuf[h - 1, x]

    def ring_step(h, carry):
        for c in range(4):
            for side in (1, 0):
                last = 8 if (c < 2) == (side == 1) else 7

                @pl.when(h <= last)
                def _():
                    arrived(row_chunk(side, h, c), nz_recv.at[(side * 8 + h - 1) * 4 + c])

                @pl.when(h < last)
                def _():
                    nz_copy(side, h, c).start()


        @pl.when(h == 7)
        def _():
            for number in range(3):
                arrived(piece(owner_of(2, core), number), far_recv.at[number])
                to_sibling(2, number).start()

        compact(h)
        return carry

    lax.fori_loop(1, PAIRS + 1, ring_step, 0)

    arrived(gu.at[pl.ds(0, 4 * GU_ROWS)], sib_recv.at[0])
    arrived(dn.at[pl.ds(0, 4)], sib_recv.at[1])
    for number in range(3):
        own_copy(number).wait()

    def chunk_step(order, carry):
        begin = (1 - order) * 4
        for pair in range(4):
            arrived(xbuf.at[begin + pair, pl.ds(0, 3)], cx_recv.at[begin + pair])

        def hidden(n, carry):
            rows_in = xbuf[pl.ds(begin, 4)].reshape(256, D)
            at = pl.multiple_of(n * 256, 256)
            gate = jnp.dot(rows_in, gu[:, pl.ds(at, 256)], preferred_element_type=F32)
            up = jnp.dot(rows_in, gu[:, pl.ds(FF + at, 256)], preferred_element_type=F32)
            inner[:, pl.ds(at, 256)] = (gate / (1.0 + jnp.exp(-gate)) * up).astype(BF16)
            return carry

        lax.fori_loop(0, FF // 256, hidden, 0)

        def outer(n, carry):
            out = jnp.dot(inner[...], dn[n], preferred_element_type=F32)
            at = pl.multiple_of(n * DN_COLS, DN_COLS)
            ybuf[pl.ds(begin, 4), :, :, pl.ds(at, DN_COLS)] = out.astype(BF16).reshape(4, NX, 16, DN_COLS)
            return carry

        lax.fori_loop(0, NDP, outer, 0, unroll=2)
        for pair in range(3, -1, -1):
            for step in (2, 1, 3):
                target = (x + step) % NX
                remote(
                    ybuf.at[begin + pair, target],
                    ret.at[begin + pair, x],
                    sent.at[YX],
                    yx_recv.at[begin + pair],
                    xpeer(step),
                ).start()
            ret[begin + pair, x] = ybuf[begin + pair, x]
        return carry

    lax.fori_loop(0, 2, chunk_step, 0)

    def keep(pair):
        arrived(ret.at[pair, pl.ds(0, 3)], yx_recv.at[pair])
        both = jnp.dot(cmat[pair], ret[pair].reshape(64, D), preferred_element_type=F32)
        part[pair] = both.reshape(2, ROWS, D)

    def sum_copy(way, t, c):
        return remote(
            rs_out.at[way, t, c], rs_in.at[way, t, c], sent.at[UP + way], ring_recv.at[(way * 8 + t) * 4 + c],
            (above, below)[way],
        )

    def sum_arrived(way, t, c):
        arrived(rs_in.at[way, t, c], ring_recv.at[(way * 8 + t) * 4 + c])

    def cols(c):
        return slice(c * FB, (c + 1) * FB)

    keep(7)
    for c in (0, 1):
        for way in range(2):
            rs_out[way, 0, 2 * way + c] = part[7, 1, :, cols(2 * way + c)].astype(BF16)
            sum_copy(way, 0, 2 * way + c).start()
    keep(6)
    for c in (0, 1):
        for way in range(2):
            rs_out[way, 1, 2 - 2 * way + c] = part[6, way, :, cols(2 - 2 * way + c)].astype(BF16)
            sum_copy(way, 1, 2 - 2 * way + c).start()

    def reduce_step(t, carry):
        def forward(way, c):
            sum_arrived(way, t - 1, c)
            rs_out[way, t, c] = (rs_in[way, t - 1, c].astype(F32) + part[7 - t, way, :, cols(c)]).astype(BF16)
            sum_copy(way, t, c).start()

        for c in (0, 1):
            for way in range(2):
                forward(way, 2 * way + c)

        @pl.when(t > 1)
        def _():
            for c in (0, 1):
                for way in range(2):
                    forward(way, 2 - 2 * way + c)

        @pl.when(t < 7)
        def _():
            keep(6 - t)

        return carry

    lax.fori_loop(1, 8, reduce_step, 0)
    square = jnp.zeros((ROWS, 1), F32)
    for c in (0, 2, 1, 3):
        total = held[:, cols(c)].astype(F32) + part[7, 0, :, cols(c)]
        for way in range(2):
            sum_arrived(way, 7, c)
            total += rs_in[way, 7, c].astype(F32)
        final = total.astype(BF16)
        stream_ref[:, cols(c)] = final
        wide = final.astype(F32)
        square += jnp.sum(wide * wide, axis=-1, keepdims=True)
    scale = lax.rsqrt(square / D + 1e-06)
    normed_ref[...] = (stream_ref[...].astype(F32) * scale * gain_final_ref[...]).astype(BF16)

    left_all(W, wbuf.at[pl.ds(0, 15)])
    left_all(A, abuf.at[pl.ds(0, 3)])
    left_all(PAIR, qbuf)
    left_all(RS, rbuf.at[pl.ds(0, 3)])
    left_all(SX, sums_out)
    left_all(GU, gu.at[pl.ds(0, 7 * GU_ROWS)])
    left_all(DN, dn.at[pl.ds(0, 7)])
    left_all(NZS, zbuf.at[pl.ds(0, 15)])
    left_all(CX, cbuf.at[pl.ds(0, 6)])
    left_all(YX, ybuf.at[pl.ds(0, 6)])
    for way in range(2):
        left_all(UP + way, xbuf.at[pl.ds(0, 5), pl.ds(0, 3)])


def block(*args):
    vmem = pl.BlockSpec(memory_space=pltpu.VMEM)
    hbm = pl.BlockSpec(memory_space=pl.ANY)
    dma = pltpu.SemaphoreType.DMA
    counts = (5, 12, 16, 6, 4, 4, 1, 6, 3, 2, 64, 8, 8, 64)
    return pl.pallas_call(
        kernel,
        out_shape=[jax.ShapeDtypeStruct((ROWS, D), BF16)] * 2,
        in_specs=[hbm] * 2 + [vmem] * 5 + [hbm] * 2 + [vmem],
        out_specs=[vmem] * 2,
        scratch_shapes=[
            pltpu.VMEM((NX, NDP * ROWS, FB), BF16),
            pltpu.VMEM((ROWS, D), BF16),
            pltpu.VMEM((NZ, ROWS, FB), BF16),
            pltpu.VMEM((NC, NY, NX, ROWS, FB), BF16),
            pltpu.VMEM((NY, NX, ROWS, FB), BF16),
            pltpu.VMEM((NY, NX, ROWS, FB), BF16),
            pltpu.VMEM((NY, NX, ROWS, FB), BF16),
            pltpu.VMEM((3, ROWS, FB), BF16),
            pltpu.VMEM((NX, ROWS, FB), BF16),
            pltpu.VMEM((NX, ROWS, FB), F32),
            pltpu.VMEM((ROWS, D), BF16),
            pltpu.VMEM((NZ, ROWS, D + 128), BF16),
            pltpu.VMEM((PAIRS, NX, 16, D), BF16),
            pltpu.VMEM((PAIRS, NX, 16, D), BF16),
            pltpu.VMEM((PAIRS, 64, 64), BF16),
            pltpu.VMEM((256, FF), BF16),
            pltpu.VMEM((PAIRS, NX, 16, D), BF16),
            pltpu.VMEM((PAIRS, NX, 16, D), BF16),
            pltpu.VMEM((PAIRS, 2, ROWS, D), F32),
            pltpu.VMEM((2, 8, 4, ROWS, FB), BF16),
            pltpu.VMEM((2, 8, 4, ROWS, FB), BF16),
            pltpu.VMEM((D, 2 * FF), BF16),
            pltpu.VMEM((NDP, FF, DN_COLS), BF16),
        ]
        + [dma((count,)) for count in counts],
        compiler_params=pltpu.CompilerParams(
            collective_id=0, has_side_effects=True, vmem_limit_bytes=56 << 20
        ),
    )(*args)


def body(
    attn,
    resid,
    w_out,
    gain_post,
    route_ids,
    route_logits,
    live_count,
    w_gate_up,
    w_down,
    gain_final,
):
    stream_out, normed_out = block(
        attn[0],
        resid[0],
        w_out.T,
        gain_post[None],
        route_ids[0].T,
        route_logits[0].T,
        live_count,
        w_gate_up[0],
        w_down[0],
        gain_final[None],
    )
    return (stream_out[None], normed_out[None])


def solution(mesh):
    placed = (
        P("expert", None, "dp"),
        P("expert", "dp", None),
        P("dp", "expert"),
        P(),
        P("expert", "dp", None),
        P("expert", "dp", None),
        P("expert", "dp"),
        P("expert", "dp", None),
        P("expert", None, "dp"),
        P(),
    )
    return jax.shard_map(
        body,
        mesh=mesh,
        in_specs=placed,
        out_specs=(P("expert", "dp", None), P("expert", "dp", None)),
        check_vma=False,
    )
```

```python
import jax
import jax.numpy as jnp
from jax import lax
from jax.experimental import pallas as pl
from jax.experimental.pallas import tpu as pltpu
from jax.sharding import PartitionSpec as P

NX, NZ, NY, NC = 4, 16, 4, 2
NDP = NY * NC
ROWS, D, FB, FF, TOP, CAP = 32, 2048, 512, 768, 8, 8
GU_ROWS, DN_COLS, CUT = D // NDP, D // NDP, 192
PAIRS = NZ // 2
CHUNKS = 4
WIDE, HALF = D // CHUNKS, CHUNKS // 2
MESH = pl.DeviceIdType.MESH
F32, BF16 = jnp.float32, jnp.bfloat16
NT = (((1,), (1,)), ((), ()))


def remote(src, dst, send_sem, recv_sem, peer):
    return pltpu.make_async_remote_copy(
        src_ref=src,
        dst_ref=dst,
        send_sem=send_sem,
        recv_sem=recv_sem,
        device_id=peer,
        device_id_type=MESH,
    )


def kernel(
    attn_ref,
    resid_ref,
    w_ref,
    gain_post_ref,
    ids_ref,
    logits_ref,
    live_ref,
    gate_up_ref,
    down_ref,
    gain_final_ref,
    stream_ref,
    normed_ref,
    abuf,
    resid,
    wbuf,
    pbuf,
    qbuf,
    sbuf,
    rbuf,
    sums_out,
    sums_in,
    sums,
    held,
    table_out,
    table_in,
    zbuf,
    cbuf,
    xbuf,
    cmat,
    inner,
    ybuf,
    ret,
    part,
    rs_out,
    rs_in,
    gu,
    dn,
    own_sem,
    sent,
    w_recv,
    a_recv,
    table_recv,
    pair_recv,
    rs_recv,
    sx_recv,
    near_recv,
    far_recv,
    sib_recv,
    nz_recv,
    cx_recv,
    yx_recv,
    ring_recv,
):
    dp = lax.axis_index("dp")
    expert = lax.axis_index("expert")
    x, z = expert // NZ, expert % NZ
    y, core = dp // NC, dp % NC
    zpeer = {step: (dp, x * NZ + (z + NZ + step) % NZ) for step in range(-7, 9) if step}
    above, below = zpeer[1], zpeer[-1]

    def xpeer(step):
        return (dp, (x + step) % NX * NZ + z)

    right, left = xpeer(1), xpeer(3)

    def ypeer(step):
        return ((y + step) % NY * NC + core, expert)

    y_up, y_down = ypeer(1), ypeer(3)
    sibling = (y * NC + 1 - core, expert)

    W, A, TABLE, PAIR, RS, SX, GU, DN, NZS, CX, YX, UP = range(12)

    def left_all(kind, ref):
        remote(ref, ref, sent.at[kind], rs_recv.at[0], right).wait_send()

    def arrived(ref, semaphore):
        remote(ref, ref, sent.at[0], semaphore, right).wait_recv()

    def local(src, dst, at):
        return pltpu.make_async_copy(src, dst, own_sem.at[at])

    attn_in = local(attn_ref, abuf.at[x], 3)
    resid_in = local(resid_ref, resid, 4)
    attn_in.start()
    resid_in.start()
    wbuf[z] = w_ref[...]

    peers = list(zpeer.values()) + [xpeer(step) for step in range(1, NX)]
    peers += [ypeer(step) for step in range(1, NY)] + [sibling]
    barrier = pltpu.get_barrier_semaphore()
    for peer in peers:
        pl.semaphore_signal(barrier, inc=1, device_id=peer, device_id_type=MESH)
    pl.semaphore_wait(barrier, len(peers))

    def z_at(side, h):
        return (z + (h if side == 0 else NZ - h)) % NZ

    jumps = {6: 6, 3: 3, 1: 1, 8: 2, 7: 1, 5: 2, 4: 1, 2: 1}

    def w_copy(side, h):
        ref = wbuf.at[z_at(side, h - jumps[h])]
        return remote(ref, ref, sent.at[W], w_recv.at[side * 8 + h - 1], zpeer[jumps[h] if side else -jumps[h]])

    def half_rows(half):
        return pl.ds(half * 128, 128)

    def a_copy(way, half):
        if way < 2:
            src, dst = attn_ref.at[half_rows(half)], abuf.at[x, half_rows(half)]
        else:
            src = dst = abuf.at[(x + (3, 1)[half]) % NX, half_rows(half)]
        peer = (right, left)[way if way < 2 else half]
        return remote(src, dst, sent.at[A], a_recv.at[way * 2 + half], peer)

    def a_arrived(way, half):
        arrived(abuf.at[(x + (3, 1, 2)[way]) % NX, half_rows(half)], a_recv.at[way * 2 + half])

    for h in (6, 3, 1):
        w_copy(1, h).start()
        w_copy(0, h).start()
    for half in range(2):
        a_copy(0, half).start()
        a_copy(1, 1 - half).start()

    def piece(owner, number):
        if number == 2:
            return dn.at[owner]
        begin = pl.multiple_of(owner * GU_ROWS, GU_ROWS)
        return gu.at[pl.ds(begin, CUT)] if number == 0 else gu.at[pl.ds(begin + CUT, GU_ROWS - CUT)]

    def own_piece(number):
        if number == 2:
            return down_ref
        return gate_up_ref.at[pl.ds(0, CUT)] if number == 0 else gate_up_ref.at[pl.ds(CUT, GU_ROWS - CUT)]

    def owner_of(step, on_core):
        return (y + step) % NY * NC + on_core

    def weight_copy(src, dst, number, recv, peer):
        return remote(src, dst, sent.at[DN if number == 2 else GU], recv, peer)

    def to_near(side, number):
        peer = (y_up, y_down)[side]
        return weight_copy(own_piece(number), piece(dp, number), number, near_recv.at[side * 3 + number], peer)

    def near_arrived(side, number):
        arrived(piece(owner_of((3, 1)[side], core), number), near_recv.at[side * 3 + number])

    def to_far(number):
        ref = piece(owner_of(3 if number == 0 else 1, core), number)
        return weight_copy(ref, ref, number, far_recv.at[number], y_up if number == 0 else y_down)

    def to_sibling(step, number):
        recv = sib_recv.at[1 if number == 2 else 0]
        owner = owner_of(step, core)
        src = piece(owner, number) if step else own_piece(number)
        return weight_copy(src, piece(owner, number), number, recv, sibling)

    def own_copy(number):
        return local(own_piece(number), piece(dp, number), number)

    for number in range(3):
        to_near(0, number).start()
        to_near(1, 2 - number).start()
    for number in range(3):
        to_sibling(0, number).start()
        own_copy(number).start()

    logits = logits_ref[...]
    raised = jnp.exp(logits - jnp.max(logits, axis=0, keepdims=True))
    probs = (raised / jnp.sum(raised, axis=0, keepdims=True)).astype(BF16)
    fold = jnp.where(
        lax.broadcasted_iota(jnp.int32, (ROWS, 128), 1) % ROWS == lax.broadcasted_iota(jnp.int32, (ROWS, 128), 0), 1.0, 0.0
    ).astype(BF16)
    ids = ids_ref[...].astype(F32).astype(BF16)
    ids_t = jnp.dot(ids, fold, preferred_element_type=F32)
    probs_t = jnp.dot(probs, fold, preferred_element_type=F32)
    lane = lax.broadcasted_iota(jnp.int32, (NZ, 128), 1)
    named = (lane // ROWS * NZ + lax.broadcasted_iota(jnp.int32, (NZ, 128), 0)).astype(F32)
    chosen = jnp.zeros((NZ, 128), F32)
    weight = jnp.zeros((NZ, 128), F32)
    for k in range(TOP):
        found = named == ids_t[k : k + 1, :]
        chosen += jnp.where(found, 1.0, 0.0)
        weight += jnp.where(found, probs_t[k : k + 1, :], 0.0)
    chosen = jnp.where(lane % ROWS < live_ref[...], chosen, 0.0)
    row_l = lax.broadcasted_iota(jnp.int32, (128, 128), 0)
    col_l = lax.broadcasted_iota(jnp.int32, (128, 128), 1)
    before = jnp.where((row_l // ROWS == col_l // ROWS) & (row_l < col_l), 1.0, 0.0).astype(BF16)
    rank = jnp.dot(chosen.astype(BF16), before, preferred_element_type=F32)
    table_out[...] = jnp.zeros((NZ, 8, 128), F32)
    table_out[:, 0, :] = jnp.where(chosen > 0.5, rank, -1.0)
    table_out[:, 1, :] = weight
    table_in[z] = table_out[z]
    for step, peer in zpeer.items():
        remote(
            table_out.at[(z + NZ + step) % NZ], table_in.at[z], sent.at[TABLE], table_recv.at[0], peer
        ).start()

    for h, onwards in ((1, (2,)), (3, (5, 4)), (6, (8, 7))):
        for side in (1, 0):
            arrived(wbuf.at[z_at(side, h)], w_recv.at[side * 8 + h - 1])
            for far in onwards:
                if far <= 7 + side:
                    w_copy(side, far).start()
        if h == 3:
            a_arrived(0, 0)
            a_copy(2, 0).start()
            a_arrived(1, 1)
            a_copy(2, 1).start()
    for h in (2, 4, 5, 7, 8):
        for side in (1, 0):
            if h <= 7 + side:
                arrived(wbuf.at[z_at(side, h)], w_recv.at[side * 8 + h - 1])
    attn_in.wait()
    resid_in.wait()
    for way, half in ((0, 1), (1, 0), (2, 0), (2, 1)):
        a_arrived(way, half)

    def product(order, carry):
        got = lax.dot_general(
            abuf[(x + 3 - order) % NX], wbuf[...].reshape(FB, FB), NT, preferred_element_type=F32
        )
        blocks = got.astype(BF16).reshape(NY, NC, ROWS, FB)
        for half in range(NC):
            pbuf[half, :, order] = blocks[:, half]
        remote(
            pbuf.at[1 - core, :, order], qbuf.at[:, order], sent.at[PAIR], pair_recv.at[order], sibling
        ).start()
        return carry

    lax.fori_loop(0, NX, product, 0)

    def exchange(order, carry):
        arrived(qbuf.at[:, order], pair_recv.at[order])
        sbuf[:, order] = (pbuf[core, :, order].astype(F32) + qbuf[:, order].astype(F32)).astype(BF16)
        for step in (2, 1, 3):
            target = (y + step) % NY
            remote(
                sbuf.at[target, order], rbuf.at[y, order], sent.at[RS], rs_recv.at[order], ypeer(step)
            ).start()
        return carry

    lax.fori_loop(0, NX, exchange, 0)

    def sum_up(order, carry):
        arrived(rbuf.at[pl.ds(0, 3), order], rs_recv.at[order])
        total = pbuf[core, y, order].astype(F32) + qbuf[y, order].astype(F32)
        for step in range(1, NY):
            total += rbuf[(y + step) % NY, order].astype(F32)

        @pl.when(order < 3)
        def _():
            sums_out[order] = total.astype(BF16)
            remote(sums_out.at[order], sums_in.at[x], sent.at[SX], sx_recv.at[0], xpeer(3 - order)).start()

        @pl.when(order == 3)
        def _():
            sums[x] = total

        return carry

    lax.fori_loop(0, NX, sum_up, 0)

    arrived(sums_in.at[pl.ds(0, 3)], sx_recv.at[0])
    for step in range(1, NX):
        source = (x + step) % NX
        sums[source] = sums_in[source].astype(F32)

    square = jnp.zeros((ROWS, 1), F32)
    for g in range(4):
        cols = slice(g * FB, (g + 1) * FB)
        both = (resid[:, cols].astype(F32) + sums[g]).astype(BF16)
        held[:, cols] = both
        wide = both.astype(F32)
        square += jnp.sum(wide * wide, axis=-1, keepdims=True)
    scale = lax.rsqrt(square / D + 1e-06)
    normed = (held[...].astype(F32) * scale * gain_post_ref[...]).astype(BF16)
    zbuf[z] = normed

    def row_chunk(side, h, c):
        return zbuf.at[z_at(side, h), :, pl.ds(c * WIDE, WIDE)]

    def nz_copy(side, h, c):
        ref = row_chunk(side, h, c)
        return remote(ref, ref, sent.at[NZS], nz_recv.at[(side * 8 + h) * CHUNKS + c], above if side else below)

    for c in range(CHUNKS):
        nz_copy(1, 0, c).start()
        nz_copy(0, 0, c).start()

    for number in range(3):
        near_arrived(0, number)
        near_arrived(1, 2 - number)
        if number == 0:
            to_far(0).start()
            to_far(2).start()
        if number == 1:
            to_far(1).start()
    for number in range(3):
        to_sibling(3, number).start()
        to_sibling(1, number).start()

    slot_i = lax.broadcasted_iota(jnp.int32, (64, 128), 0)
    slot_l = lax.broadcasted_iota(jnp.int32, (64, 128), 1)
    slot_k = (slot_i % CAP).astype(F32)
    slot_x = slot_l // ROWS == slot_i // 16
    slot_side = [slot_x & (slot_i // CAP % 2 == side) for side in range(2)]
    arrived(table_in.at[pl.ds(0, NZ - 1)], table_recv.at[0])

    def compact(h):
        total = jnp.zeros((64, D), F32)
        for side, source in enumerate((z_at(0, h % PAIRS), z_at(1, h))):
            hit = slot_side[side] & (table_in[source, 0:1, :] == slot_k)
            picked = jnp.where(hit, 1.0, 0.0).astype(BF16)
            choose = lax.dot_general(picked, fold, NT, preferred_element_type=F32).astype(BF16)
            scaled = jnp.where(hit, table_in[source, 1:2, :], 0.0).astype(BF16)
            spread = lax.dot_general(fold, scaled, NT, preferred_element_type=F32)
            cmat[h - 1, side * ROWS : (side + 1) * ROWS] = spread.astype(BF16)
            total += jnp.dot(choose, zbuf[source], preferred_element_type=F32)
        cbuf[h - 1] = total.astype(BF16).reshape(NX, 16, D)
        for step in (2, 1, 3):
            target = (x + step) % NX
            remote(
                cbuf.at[h - 1, target], xbuf.at[h - 1, x], sent.at[CX], cx_recv.at[h - 1], xpeer(step)
            ).start()
        xbuf[h - 1, x] = cbuf[h - 1, x]

    def ring_step(h, carry):
        for c in range(CHUNKS):
            for side in (1, 0):
                last = 8 if (c < HALF) == (side == 1) else 7

                @pl.when(h <= last)
                def _():
                    arrived(row_chunk(side, h, c), nz_recv.at[(side * 8 + h - 1) * CHUNKS + c])

                @pl.when(h < last)
                def _():
                    nz_copy(side, h, c).start()


        @pl.when(h == 7)
        def _():
            for number in range(3):
                arrived(piece(owner_of(2, core), number), far_recv.at[number])
                to_sibling(2, number).start()

        compact(h)
        return carry

    lax.fori_loop(1, PAIRS + 1, ring_step, 0)

    arrived(gu.at[pl.ds(0, 4 * GU_ROWS)], sib_recv.at[0])
    arrived(dn.at[pl.ds(0, 4)], sib_recv.at[1])
    for number in range(3):
        own_copy(number).wait()

    def experts(begin, count):
        rows = count * 64
        for pair in range(count):
            arrived(xbuf.at[begin + pair, pl.ds(0, 3)], cx_recv.at[begin + pair])

        def hidden(n, carry):
            rows_in = xbuf[pl.ds(begin, count)].reshape(rows, D)
            at = pl.multiple_of(n * 256, 256)
            gate = jnp.dot(rows_in, gu[:, pl.ds(at, 256)], preferred_element_type=F32)
            up = jnp.dot(rows_in, gu[:, pl.ds(FF + at, 256)], preferred_element_type=F32)
            inner[0:rows, pl.ds(at, 256)] = (gate / (1.0 + jnp.exp(-gate)) * up).astype(BF16)
            return carry

        lax.fori_loop(0, FF // 256, hidden, 0)

        def outer(n, carry):
            out = jnp.dot(inner[0:rows], dn[n], preferred_element_type=F32)
            at = pl.multiple_of(n * DN_COLS, DN_COLS)
            ybuf[pl.ds(begin, count), :, :, pl.ds(at, DN_COLS)] = out.astype(BF16).reshape(count, NX, 16, DN_COLS)
            return carry

        lax.fori_loop(0, NDP, outer, 0, unroll=4)

    def give_back(pair):
        for step in (2, 1, 3):
            target = (x + step) % NX
            remote(
                ybuf.at[pair, target], ret.at[pair, x], sent.at[YX], yx_recv.at[pair], xpeer(step)
            ).start()
        ret[pair, x] = ybuf[pair, x]

    experts(0, 4)

    def chunk_step(order, carry):
        begin = 6 - 2 * order
        experts(begin, 2)
        give_back(begin + 1)
        give_back(begin)
        return carry

    lax.fori_loop(0, 2, chunk_step, 0)
    for pair in (3, 2, 1, 0):
        give_back(pair)

    def keep(pair):
        arrived(ret.at[pair, pl.ds(0, 3)], yx_recv.at[pair])
        both = jnp.dot(cmat[pair], ret[pair].reshape(64, D), preferred_element_type=F32)
        part[pair] = both.reshape(2, ROWS, D)

    def sum_copy(way, t, c):
        return remote(
            rs_out.at[way, t, c], rs_in.at[way, t, c], sent.at[UP + way], ring_recv.at[(way * 8 + t) * CHUNKS + c],
            (above, below)[way],
        )

    def sum_arrived(way, t, c):
        arrived(rs_in.at[way, t, c], ring_recv.at[(way * 8 + t) * CHUNKS + c])

    def cols(c):
        return slice(c * WIDE, (c + 1) * WIDE)

    keep(7)
    for c in range(HALF):
        for way in range(2):
            rs_out[way, 0, HALF * way + c] = part[7, 1, :, cols(HALF * way + c)].astype(BF16)
            sum_copy(way, 0, HALF * way + c).start()
    keep(6)
    for c in range(HALF):
        for way in range(2):
            rs_out[way, 1, HALF * (1 - way) + c] = part[6, way, :, cols(HALF * (1 - way) + c)].astype(BF16)
            sum_copy(way, 1, HALF * (1 - way) + c).start()

    def reduce_step(t, carry):
        def forward(way, c):
            sum_arrived(way, t - 1, c)
            rs_out[way, t, c] = (rs_in[way, t - 1, c].astype(F32) + part[7 - t, way, :, cols(c)]).astype(BF16)
            sum_copy(way, t, c).start()

        for c in range(HALF):
            for way in range(2):
                forward(way, HALF * way + c)

        @pl.when(t > 1)
        def _():
            for c in range(HALF):
                for way in range(2):
                    forward(way, HALF * (1 - way) + c)

        @pl.when(t < 7)
        def _():
            keep(6 - t)

        return carry

    lax.fori_loop(1, 8, reduce_step, 0)
    square = jnp.zeros((ROWS, 1), F32)
    for c in range(CHUNKS):
        total = held[:, cols(c)].astype(F32) + part[7, 0, :, cols(c)]
        for way in range(2):
            sum_arrived(way, 7, c)
            total += rs_in[way, 7, c].astype(F32)
        final = total.astype(BF16)
        stream_ref[:, cols(c)] = final
        wide = final.astype(F32)
        square += jnp.sum(wide * wide, axis=-1, keepdims=True)
    scale = lax.rsqrt(square / D + 1e-06)
    normed_ref[...] = (stream_ref[...].astype(F32) * scale * gain_final_ref[...]).astype(BF16)

    left_all(W, wbuf.at[pl.ds(0, 15)])
    left_all(A, abuf.at[pl.ds(0, 3)])
    left_all(TABLE, table_out.at[pl.ds(0, NZ - 1)])
    left_all(PAIR, qbuf)
    left_all(RS, rbuf.at[pl.ds(0, 3)])
    left_all(SX, sums_out)
    left_all(GU, gu.at[pl.ds(0, 7 * GU_ROWS)])
    left_all(DN, dn.at[pl.ds(0, 7)])
    left_all(NZS, zbuf.at[pl.ds(0, 15)])
    left_all(CX, cbuf.at[pl.ds(0, 6)])
    left_all(YX, ybuf.at[pl.ds(0, 6)])
    for way in range(2):
        left_all(UP + way, xbuf.at[pl.ds(0, 5), pl.ds(0, 3)])


def block(*args):
    vmem = pl.BlockSpec(memory_space=pltpu.VMEM)
    hbm = pl.BlockSpec(memory_space=pl.ANY)
    dma = pltpu.SemaphoreType.DMA
    counts = (5, 13, 16, 6, 1, 4, 4, 1, 6, 3, 2, 16 * CHUNKS, 8, 8, 16 * CHUNKS)
    return pl.pallas_call(
        kernel,
        out_shape=[jax.ShapeDtypeStruct((ROWS, D), BF16)] * 2,
        in_specs=[hbm] * 2 + [vmem] * 5 + [hbm] * 2 + [vmem],
        out_specs=[vmem] * 2,
        scratch_shapes=[
            pltpu.VMEM((NX, NDP * ROWS, FB), BF16),
            pltpu.VMEM((ROWS, D), BF16),
            pltpu.VMEM((NZ, ROWS, FB), BF16),
            pltpu.VMEM((NC, NY, NX, ROWS, FB), BF16),
            pltpu.VMEM((NY, NX, ROWS, FB), BF16),
            pltpu.VMEM((NY, NX, ROWS, FB), BF16),
            pltpu.VMEM((NY, NX, ROWS, FB), BF16),
            pltpu.VMEM((3, ROWS, FB), BF16),
            pltpu.VMEM((NX, ROWS, FB), BF16),
            pltpu.VMEM((NX, ROWS, FB), F32),
            pltpu.VMEM((ROWS, D), BF16),
            pltpu.VMEM((NZ, 8, 128), F32),
            pltpu.VMEM((NZ, 8, 128), F32),
            pltpu.VMEM((NZ, ROWS, D), BF16),
            pltpu.VMEM((PAIRS, NX, 16, D), BF16),
            pltpu.VMEM((PAIRS, NX, 16, D), BF16),
            pltpu.VMEM((PAIRS, 64, 64), BF16),
            pltpu.VMEM((256, FF), BF16),
            pltpu.VMEM((PAIRS, NX, 16, D), BF16),
            pltpu.VMEM((PAIRS, NX, 16, D), BF16),
            pltpu.VMEM((PAIRS, 2, ROWS, D), F32),
            pltpu.VMEM((2, 8, CHUNKS, ROWS, WIDE), BF16),
            pltpu.VMEM((2, 8, CHUNKS, ROWS, WIDE), BF16),
            pltpu.VMEM((D, 2 * FF), BF16),
            pltpu.VMEM((NDP, FF, DN_COLS), BF16),
        ]
        + [dma((count,)) for count in counts],
        compiler_params=pltpu.CompilerParams(
            collective_id=0, has_side_effects=True, vmem_limit_bytes=56 << 20
        ),
    )(*args)


def body(
    attn,
    resid,
    w_out,
    gain_post,
    route_ids,
    route_logits,
    live_count,
    w_gate_up,
    w_down,
    gain_final,
):
    stream_out, normed_out = block(
        attn[0],
        resid[0],
        w_out.T,
        gain_post[None],
        route_ids[0].T,
        route_logits[0].T,
        live_count,
        w_gate_up[0],
        w_down[0],
        gain_final[None],
    )
    return (stream_out[None], normed_out[None])


def solution(mesh):
    placed = (
        P("expert", None, "dp"),
        P("expert", "dp", None),
        P("dp", "expert"),
        P(),
        P("expert", "dp", None),
        P("expert", "dp", None),
        P("expert", "dp"),
        P("expert", "dp", None),
        P("expert", None, "dp"),
        P(),
    )
    return jax.shard_map(
        body,
        mesh=mesh,
        in_specs=placed,
        out_specs=(P("expert", "dp", None), P("expert", "dp", None)),
        check_vma=False,
    )
```

```python
import jax
import jax.numpy as jnp
from jax import lax
from jax.experimental import pallas as pl
from jax.experimental.pallas import tpu as pltpu
from jax.sharding import PartitionSpec as P

NX, NZ, NY, NC = 4, 16, 4, 2
NDP = NY * NC
ROWS, D, FB, FF, TOP, CAP = 32, 2048, 512, 768, 8, 8
GU_ROWS, DN_COLS, CUT = D // NDP, D // NDP, 192
PAIRS = NZ // 2
CHUNKS = 4
WIDE, HALF = D // CHUNKS, CHUNKS // 2
MESH = pl.DeviceIdType.MESH
F32, BF16 = jnp.float32, jnp.bfloat16
NT = (((1,), (1,)), ((), ()))


def remote(src, dst, send_sem, recv_sem, peer):
    return pltpu.make_async_remote_copy(
        src_ref=src,
        dst_ref=dst,
        send_sem=send_sem,
        recv_sem=recv_sem,
        device_id=peer,
        device_id_type=MESH,
    )


def kernel(
    attn_ref,
    resid_ref,
    w_ref,
    gain_post_ref,
    ids_ref,
    logits_ref,
    live_ref,
    gate_up_ref,
    down_ref,
    gain_final_ref,
    stream_ref,
    normed_ref,
    abuf,
    resid,
    wbuf,
    pbuf,
    qbuf,
    sbuf,
    rbuf,
    sums_out,
    sums_in,
    sums,
    held,
    table_out,
    table_in,
    zbuf,
    cbuf,
    xbuf,
    cmat,
    inner,
    ybuf,
    ret,
    part,
    rs_out,
    rs_in,
    gu,
    dn,
    own_sem,
    sent,
    w_recv,
    a_recv,
    table_recv,
    pair_recv,
    rs_recv,
    sx_recv,
    near_recv,
    far_recv,
    sib_recv,
    nz_recv,
    cx_recv,
    yx_recv,
    ring_recv,
):
    dp = lax.axis_index("dp")
    expert = lax.axis_index("expert")
    x, z = expert // NZ, expert % NZ
    y, core = dp // NC, dp % NC
    zpeer = {step: (dp, x * NZ + (z + NZ + step) % NZ) for step in range(-7, 9) if step}
    above, below = zpeer[1], zpeer[-1]

    def xpeer(step):
        return (dp, (x + step) % NX * NZ + z)

    right, left = xpeer(1), xpeer(3)

    def ypeer(step):
        return ((y + step) % NY * NC + core, expert)

    y_up, y_down = ypeer(1), ypeer(3)
    sibling = (y * NC + 1 - core, expert)

    W, A, TABLE, PAIR, RS, SX, GU, DN, NZS, CX, YX, UP = range(12)

    def left_all(kind, ref):
        remote(ref, ref, sent.at[kind], rs_recv.at[0], right).wait_send()

    def arrived(ref, semaphore):
        remote(ref, ref, sent.at[0], semaphore, right).wait_recv()

    def local(src, dst, at):
        return pltpu.make_async_copy(src, dst, own_sem.at[at])

    attn_in = local(attn_ref, abuf.at[x], 3)
    resid_in = local(resid_ref, resid, 4)
    attn_in.start()
    resid_in.start()
    wbuf[z] = w_ref[...]

    peers = list(zpeer.values()) + [xpeer(step) for step in range(1, NX)]
    peers += [ypeer(step) for step in range(1, NY)] + [sibling]
    barrier = pltpu.get_barrier_semaphore()
    for peer in peers:
        pl.semaphore_signal(barrier, inc=1, device_id=peer, device_id_type=MESH)
    pl.semaphore_wait(barrier, len(peers))

    def z_at(side, h):
        return (z + (h if side == 0 else NZ - h)) % NZ

    jumps = {6: 6, 3: 3, 1: 1, 8: 2, 7: 1, 5: 2, 4: 1, 2: 1}

    def w_copy(side, h):
        ref = wbuf.at[z_at(side, h - jumps[h])]
        return remote(ref, ref, sent.at[W], w_recv.at[side * 8 + h - 1], zpeer[jumps[h] if side else -jumps[h]])

    def half_rows(half):
        return pl.ds(half * 128, 128)

    def a_copy(way, half):
        if way < 2:
            src, dst = attn_ref.at[half_rows(half)], abuf.at[x, half_rows(half)]
        else:
            src = dst = abuf.at[(x + (3, 1)[half]) % NX, half_rows(half)]
        peer = (right, left)[way if way < 2 else half]
        return remote(src, dst, sent.at[A], a_recv.at[way * 2 + half], peer)

    def a_arrived(way, half):
        arrived(abuf.at[(x + (3, 1, 2)[way]) % NX, half_rows(half)], a_recv.at[way * 2 + half])

    for h in (6, 3, 1):
        w_copy(1, h).start()
        w_copy(0, h).start()
    for half in range(2):
        a_copy(0, half).start()
        a_copy(1, 1 - half).start()

    def piece(owner, number):
        if number == 2:
            return dn.at[owner]
        begin = pl.multiple_of(owner * GU_ROWS, GU_ROWS)
        return gu.at[pl.ds(begin, CUT)] if number == 0 else gu.at[pl.ds(begin + CUT, GU_ROWS - CUT)]

    def own_piece(number):
        if number == 2:
            return down_ref
        return gate_up_ref.at[pl.ds(0, CUT)] if number == 0 else gate_up_ref.at[pl.ds(CUT, GU_ROWS - CUT)]

    def owner_of(step, on_core):
        return (y + step) % NY * NC + on_core

    def weight_copy(src, dst, number, recv, peer):
        return remote(src, dst, sent.at[DN if number == 2 else GU], recv, peer)

    def to_near(side, number):
        peer = (y_up, y_down)[side]
        return weight_copy(own_piece(number), piece(dp, number), number, near_recv.at[side * 3 + number], peer)

    def near_arrived(side, number):
        arrived(piece(owner_of((3, 1)[side], core), number), near_recv.at[side * 3 + number])

    def to_far(number):
        ref = piece(owner_of(3 if number == 0 else 1, core), number)
        return weight_copy(ref, ref, number, far_recv.at[number], y_up if number == 0 else y_down)

    def to_sibling(step, number):
        recv = sib_recv.at[1 if number == 2 else 0]
        owner = owner_of(step, core)
        src = piece(owner, number) if step else own_piece(number)
        return weight_copy(src, piece(owner, number), number, recv, sibling)

    def own_copy(number):
        return local(own_piece(number), piece(dp, number), number)

    for number in range(2):
        to_near(0, number).start()
        to_near(1, 1 - number).start()
    for number in range(3):
        to_sibling(0, number).start()
        own_copy(number).start()

    logits = logits_ref[...]
    raised = jnp.exp(logits - jnp.max(logits, axis=0, keepdims=True))
    probs = (raised / jnp.sum(raised, axis=0, keepdims=True)).astype(BF16)
    fold = jnp.where(
        lax.broadcasted_iota(jnp.int32, (ROWS, 128), 1) % ROWS == lax.broadcasted_iota(jnp.int32, (ROWS, 128), 0), 1.0, 0.0
    ).astype(BF16)
    ids = ids_ref[...].astype(F32).astype(BF16)
    ids_t = jnp.dot(ids, fold, preferred_element_type=F32)
    probs_t = jnp.dot(probs, fold, preferred_element_type=F32)
    lane = lax.broadcasted_iota(jnp.int32, (NZ, 128), 1)
    named = (lane // ROWS * NZ + lax.broadcasted_iota(jnp.int32, (NZ, 128), 0)).astype(F32)
    chosen = jnp.zeros((NZ, 128), F32)
    weight = jnp.zeros((NZ, 128), F32)
    for k in range(TOP):
        found = named == ids_t[k : k + 1, :]
        chosen += jnp.where(found, 1.0, 0.0)
        weight += jnp.where(found, probs_t[k : k + 1, :], 0.0)
    chosen = jnp.where(lane % ROWS < live_ref[...], chosen, 0.0)
    row_l = lax.broadcasted_iota(jnp.int32, (128, 128), 0)
    col_l = lax.broadcasted_iota(jnp.int32, (128, 128), 1)
    before = jnp.where((row_l // ROWS == col_l // ROWS) & (row_l < col_l), 1.0, 0.0).astype(BF16)
    rank = jnp.dot(chosen.astype(BF16), before, preferred_element_type=F32)
    table_out[...] = jnp.zeros((NZ, 8, 128), F32)
    table_out[:, 0, :] = jnp.where(chosen > 0.5, rank, -1.0)
    table_out[:, 1, :] = weight
    table_in[z] = table_out[z]
    for step, peer in zpeer.items():
        remote(
            table_out.at[(z + NZ + step) % NZ], table_in.at[z], sent.at[TABLE], table_recv.at[0], peer
        ).start()

    for h, onwards in ((1, (2,)), (3, (5, 4)), (6, (8, 7))):
        for side in (1, 0):
            arrived(wbuf.at[z_at(side, h)], w_recv.at[side * 8 + h - 1])
            for far in onwards:
                if far <= 7 + side:
                    w_copy(side, far).start()
        if h == 3:
            a_arrived(0, 0)
            a_copy(2, 0).start()
            a_arrived(1, 1)
            a_copy(2, 1).start()
    for h in (2, 4, 5, 7, 8):
        for side in (1, 0):
            if h <= 7 + side:
                arrived(wbuf.at[z_at(side, h)], w_recv.at[side * 8 + h - 1])
    attn_in.wait()
    resid_in.wait()
    for way, half in ((0, 1), (1, 0), (2, 0), (2, 1)):
        a_arrived(way, half)

    def product(order, carry):
        got = lax.dot_general(
            abuf[(x + 3 - order) % NX], wbuf[...].reshape(FB, FB), NT, preferred_element_type=F32
        )
        blocks = got.astype(BF16).reshape(NY, NC, ROWS, FB)
        for half in range(NC):
            pbuf[half, :, order] = blocks[:, half]
        remote(
            pbuf.at[1 - core, :, order], qbuf.at[:, order], sent.at[PAIR], pair_recv.at[order], sibling
        ).start()
        return carry

    lax.fori_loop(0, NX, product, 0)

    def exchange(order, carry):
        arrived(qbuf.at[:, order], pair_recv.at[order])
        sbuf[:, order] = (pbuf[core, :, order].astype(F32) + qbuf[:, order].astype(F32)).astype(BF16)
        for step in (2, 1, 3):
            target = (y + step) % NY
            remote(
                sbuf.at[target, order], rbuf.at[y, order], sent.at[RS], rs_recv.at[order], ypeer(step)
            ).start()
        return carry

    lax.fori_loop(0, NX, exchange, 0)
    to_near(0, 2).start()
    to_near(1, 2).start()

    def sum_up(order, carry):
        arrived(rbuf.at[pl.ds(0, 3), order], rs_recv.at[order])
        total = pbuf[core, y, order].astype(F32) + qbuf[y, order].astype(F32)
        for step in range(1, NY):
            total += rbuf[(y + step) % NY, order].astype(F32)

        @pl.when(order < 3)
        def _():
            sums_out[order] = total.astype(BF16)
            remote(sums_out.at[order], sums_in.at[x], sent.at[SX], sx_recv.at[0], xpeer(3 - order)).start()

        @pl.when(order == 3)
        def _():
            sums[x] = total

        return carry

    lax.fori_loop(0, NX, sum_up, 0)

    arrived(sums_in.at[pl.ds(0, 3)], sx_recv.at[0])
    for step in range(1, NX):
        source = (x + step) % NX
        sums[source] = sums_in[source].astype(F32)

    square = jnp.zeros((ROWS, 1), F32)
    for g in range(4):
        cols = slice(g * FB, (g + 1) * FB)
        both = (resid[:, cols].astype(F32) + sums[g]).astype(BF16)
        held[:, cols] = both
        wide = both.astype(F32)
        square += jnp.sum(wide * wide, axis=-1, keepdims=True)
    scale = lax.rsqrt(square / D + 1e-06)
    normed = (held[...].astype(F32) * scale * gain_post_ref[...]).astype(BF16)
    zbuf[z] = normed

    def row_chunk(side, h, c):
        return zbuf.at[z_at(side, h), :, pl.ds(c * WIDE, WIDE)]

    def nz_copy(side, h, c):
        ref = row_chunk(side, h, c)
        return remote(ref, ref, sent.at[NZS], nz_recv.at[(side * 8 + h) * CHUNKS + c], above if side else below)

    for c in range(CHUNKS):
        nz_copy(1, 0, c).start()
        nz_copy(0, 0, c).start()

    for number in range(3):
        near_arrived(0, number)
        near_arrived(1, 2 - number)
        if number == 0:
            to_far(0).start()
            to_far(2).start()
        if number == 1:
            to_far(1).start()
    for number in range(3):
        to_sibling(3, number).start()
        to_sibling(1, number).start()

    slot_i = lax.broadcasted_iota(jnp.int32, (64, 128), 0)
    slot_l = lax.broadcasted_iota(jnp.int32, (64, 128), 1)
    slot_k = (slot_i % CAP).astype(F32)
    slot_x = slot_l // ROWS == slot_i // 16
    slot_side = [slot_x & (slot_i // CAP % 2 == side) for side in range(2)]
    arrived(table_in.at[pl.ds(0, NZ - 1)], table_recv.at[0])

    def compact(h):
        total = jnp.zeros((64, D), F32)
        for side, source in enumerate((z_at(0, h % PAIRS), z_at(1, h))):
            hit = slot_side[side] & (table_in[source, 0:1, :] == slot_k)
            picked = jnp.where(hit, 1.0, 0.0).astype(BF16)
            choose = lax.dot_general(picked, fold, NT, preferred_element_type=F32).astype(BF16)
            scaled = jnp.where(hit, table_in[source, 1:2, :], 0.0).astype(BF16)
            spread = lax.dot_general(fold, scaled, NT, preferred_element_type=F32)
            cmat[h - 1, side * ROWS : (side + 1) * ROWS] = spread.astype(BF16)
            total += jnp.dot(choose, zbuf[source], preferred_element_type=F32)
        cbuf[h - 1] = total.astype(BF16).reshape(NX, 16, D)
        for step in (2, 1, 3):
            target = (x + step) % NX
            remote(
                cbuf.at[h - 1, target], xbuf.at[h - 1, x], sent.at[CX], cx_recv.at[h - 1], xpeer(step)
            ).start()
        xbuf[h - 1, x] = cbuf[h - 1, x]

    def ring_step(h, carry):
        for c in range(CHUNKS):
            for side in (1, 0):
                last = 8 if (c < HALF) == (side == 1) else 7

                @pl.when(h <= last)
                def _():
                    arrived(row_chunk(side, h, c), nz_recv.at[(side * 8 + h - 1) * CHUNKS + c])

                @pl.when(h < last)
                def _():
                    nz_copy(side, h, c).start()


        @pl.when(h == 7)
        def _():
            for number in range(3):
                arrived(piece(owner_of(2, core), number), far_recv.at[number])
                to_sibling(2, number).start()

        compact(h)
        return carry

    lax.fori_loop(1, PAIRS + 1, ring_step, 0)

    arrived(gu.at[pl.ds(0, 4 * GU_ROWS)], sib_recv.at[0])
    arrived(dn.at[pl.ds(0, 4)], sib_recv.at[1])
    for number in range(3):
        own_copy(number).wait()

    def experts(begin, count):
        rows = count * 64
        for pair in range(count):
            arrived(xbuf.at[begin + pair, pl.ds(0, 3)], cx_recv.at[begin + pair])

        def hidden(n, carry):
            rows_in = xbuf[pl.ds(begin, count)].reshape(rows, D)
            at = pl.multiple_of(n * 256, 256)
            gate = jnp.dot(rows_in, gu[:, pl.ds(at, 256)], preferred_element_type=F32)
            up = jnp.dot(rows_in, gu[:, pl.ds(FF + at, 256)], preferred_element_type=F32)
            inner[0:rows, pl.ds(at, 256)] = (gate / (1.0 + jnp.exp(-gate)) * up).astype(BF16)
            return carry

        lax.fori_loop(0, FF // 256, hidden, 0)

        def outer(n, carry):
            out = jnp.dot(inner[0:rows], dn[n], preferred_element_type=F32)
            at = pl.multiple_of(n * DN_COLS, DN_COLS)
            ybuf[pl.ds(begin, count), :, :, pl.ds(at, DN_COLS)] = out.astype(BF16).reshape(count, NX, 16, DN_COLS)
            return carry

        lax.fori_loop(0, NDP, outer, 0, unroll=4)

    def give_back(pair):
        for step in (2, 1, 3):
            target = (x + step) % NX
            remote(
                ybuf.at[pair, target], ret.at[pair, x], sent.at[YX], yx_recv.at[pair], xpeer(step)
            ).start()
        ret[pair, x] = ybuf[pair, x]

    experts(0, 4)

    def chunk_step(order, carry):
        begin = 6 - 2 * order
        experts(begin, 2)
        give_back(begin + 1)
        give_back(begin)
        return carry

    lax.fori_loop(0, 2, chunk_step, 0)
    for pair in (3, 2, 1, 0):
        give_back(pair)

    def keep(pair):
        arrived(ret.at[pair, pl.ds(0, 3)], yx_recv.at[pair])
        both = jnp.dot(cmat[pair], ret[pair].reshape(64, D), preferred_element_type=F32)
        part[pair] = both.reshape(2, ROWS, D)

    def sum_copy(way, t, c):
        return remote(
            rs_out.at[way, t, c], rs_in.at[way, t, c], sent.at[UP + way], ring_recv.at[(way * 8 + t) * CHUNKS + c],
            (above, below)[way],
        )

    def sum_arrived(way, t, c):
        arrived(rs_in.at[way, t, c], ring_recv.at[(way * 8 + t) * CHUNKS + c])

    def cols(c):
        return slice(c * WIDE, (c + 1) * WIDE)

    keep(7)
    for c in range(HALF):
        for way in range(2):
            rs_out[way, 0, HALF * way + c] = part[7, 1, :, cols(HALF * way + c)].astype(BF16)
            sum_copy(way, 0, HALF * way + c).start()
    keep(6)
    for c in range(HALF):
        for way in range(2):
            rs_out[way, 1, HALF * (1 - way) + c] = part[6, way, :, cols(HALF * (1 - way) + c)].astype(BF16)
            sum_copy(way, 1, HALF * (1 - way) + c).start()

    def reduce_step(t, carry):
        def forward(way, c):
            sum_arrived(way, t - 1, c)
            rs_out[way, t, c] = (rs_in[way, t - 1, c].astype(F32) + part[7 - t, way, :, cols(c)]).astype(BF16)
            sum_copy(way, t, c).start()

        for c in range(HALF):
            for way in range(2):
                forward(way, HALF * way + c)

        @pl.when(t > 1)
        def _():
            for c in range(HALF):
                for way in range(2):
                    forward(way, HALF * (1 - way) + c)

        @pl.when(t < 7)
        def _():
            keep(6 - t)

        return carry

    lax.fori_loop(1, 8, reduce_step, 0)
    square = jnp.zeros((ROWS, 1), F32)
    for c in range(CHUNKS):
        total = held[:, cols(c)].astype(F32) + part[7, 0, :, cols(c)]
        for way in range(2):
            sum_arrived(way, 7, c)
            total += rs_in[way, 7, c].astype(F32)
        final = total.astype(BF16)
        stream_ref[:, cols(c)] = final
        wide = final.astype(F32)
        square += jnp.sum(wide * wide, axis=-1, keepdims=True)
    scale = lax.rsqrt(square / D + 1e-06)
    normed_ref[...] = (stream_ref[...].astype(F32) * scale * gain_final_ref[...]).astype(BF16)

    left_all(W, wbuf.at[pl.ds(0, 15)])
    left_all(A, abuf.at[pl.ds(0, 3)])
    left_all(TABLE, table_out.at[pl.ds(0, NZ - 1)])
    left_all(PAIR, qbuf)
    left_all(RS, rbuf.at[pl.ds(0, 3)])
    left_all(SX, sums_out)
    left_all(GU, gu.at[pl.ds(0, 7 * GU_ROWS)])
    left_all(DN, dn.at[pl.ds(0, 7)])
    left_all(NZS, zbuf.at[pl.ds(0, 15)])
    left_all(CX, cbuf.at[pl.ds(0, 6)])
    left_all(YX, ybuf.at[pl.ds(0, 6)])
    for way in range(2):
        left_all(UP + way, xbuf.at[pl.ds(0, 5), pl.ds(0, 3)])


def block(*args):
    vmem = pl.BlockSpec(memory_space=pltpu.VMEM)
    hbm = pl.BlockSpec(memory_space=pl.ANY)
    dma = pltpu.SemaphoreType.DMA
    counts = (5, 13, 16, 6, 1, 4, 4, 1, 6, 3, 2, 16 * CHUNKS, 8, 8, 16 * CHUNKS)
    return pl.pallas_call(
        kernel,
        out_shape=[jax.ShapeDtypeStruct((ROWS, D), BF16)] * 2,
        in_specs=[hbm] * 2 + [vmem] * 5 + [hbm] * 2 + [vmem],
        out_specs=[vmem] * 2,
        scratch_shapes=[
            pltpu.VMEM((NX, NDP * ROWS, FB), BF16),
            pltpu.VMEM((ROWS, D), BF16),
            pltpu.VMEM((NZ, ROWS, FB), BF16),
            pltpu.VMEM((NC, NY, NX, ROWS, FB), BF16),
            pltpu.VMEM((NY, NX, ROWS, FB), BF16),
            pltpu.VMEM((NY, NX, ROWS, FB), BF16),
            pltpu.VMEM((NY, NX, ROWS, FB), BF16),
            pltpu.VMEM((3, ROWS, FB), BF16),
            pltpu.VMEM((NX, ROWS, FB), BF16),
            pltpu.VMEM((NX, ROWS, FB), F32),
            pltpu.VMEM((ROWS, D), BF16),
            pltpu.VMEM((NZ, 8, 128), F32),
            pltpu.VMEM((NZ, 8, 128), F32),
            pltpu.VMEM((NZ, ROWS, D), BF16),
            pltpu.VMEM((PAIRS, NX, 16, D), BF16),
            pltpu.VMEM((PAIRS, NX, 16, D), BF16),
            pltpu.VMEM((PAIRS, 64, 64), BF16),
            pltpu.VMEM((256, FF), BF16),
            pltpu.VMEM((PAIRS, NX, 16, D), BF16),
            pltpu.VMEM((PAIRS, NX, 16, D), BF16),
            pltpu.VMEM((PAIRS, 2, ROWS, D), F32),
            pltpu.VMEM((2, 8, CHUNKS, ROWS, WIDE), BF16),
            pltpu.VMEM((2, 8, CHUNKS, ROWS, WIDE), BF16),
            pltpu.VMEM((D, 2 * FF), BF16),
            pltpu.VMEM((NDP, FF, DN_COLS), BF16),
        ]
        + [dma((count,)) for count in counts],
        compiler_params=pltpu.CompilerParams(
            collective_id=0, has_side_effects=True, vmem_limit_bytes=56 << 20
        ),
    )(*args)


def body(
    attn,
    resid,
    w_out,
    gain_post,
    route_ids,
    route_logits,
    live_count,
    w_gate_up,
    w_down,
    gain_final,
):
    stream_out, normed_out = block(
        attn[0],
        resid[0],
        w_out.T,
        gain_post[None],
        route_ids[0].T,
        route_logits[0].T,
        live_count,
        w_gate_up[0],
        w_down[0],
        gain_final[None],
    )
    return (stream_out[None], normed_out[None])


def solution(mesh):
    placed = (
        P("expert", None, "dp"),
        P("expert", "dp", None),
        P("dp", "expert"),
        P(),
        P("expert", "dp", None),
        P("expert", "dp", None),
        P("expert", "dp"),
        P("expert", "dp", None),
        P("expert", None, "dp"),
        P(),
    )
    return jax.shard_map(
        body,
        mesh=mesh,
        in_specs=placed,
        out_specs=(P("expert", "dp", None), P("expert", "dp", None)),
        check_vma=False,
    )
```
